1024 devices in a mesh: space: 64 (over z, core), vel: 16 (over y, x).
Axes of the slice: x: 4, y: 4, z: 32, core: 2. Of those that a mesh axis runs over, the one named last changes fastest.
Arguments:
- dist: float32 [64, 512, 4096], P('space', None, 'vel'), may hold values from 0.1 to 10
- neighbours: int32 [64, 6], P('space'), may hold values from -1 to 63, as said below
- solid: int32 [64, 512], P('space'), may hold values 0 or 1
Outputs:
- final_dist: float32 [64, 512, 4096], P('space', None, 'vel')
The draws below stay inside these ranges and needn't reach their ends.
Inputs may be any that keep to these rules, and one draw needn't show every extreme that they name: `neighbours`: each entry is -1 or a block held by the same index of space as block b (blocks b * 1 onwards) or by the index just below or just above it, cyclically over the space axis.
All inputs are finite; a program needn't handle non-finite values. No bound on the sum of `solid` on one device may be relied on, other than what follows from the above.
Results may differ from the reference program's by a relative error of at most 0.0003.
Values sent between devices are 32-bit elements; how exact they have to be, the bound alone decides.
No kernel may reach another device: no remote copies, remote signals or barrier semaphores. Data moves between devices by JAX's collectives and lax.ppermute only.
A program may use at most 32 MiB of HBM per device.

```python
import math
import jax
import jax.numpy as jnp
from jax import lax

NVX = 16
NV = 4096
BS = 8
CELLS = 512
BLK_DEV = 1
ITERS = 2
BLOCKS = 64


def draw_neighbours(key, part):
    key_offset, key_open = jax.random.split(jax.random.fold_in(key, 7))
    rows = jnp.arange(BLOCKS, dtype=jnp.int32)[:, None]
    offset = jax.random.randint(key_offset, (BLOCKS, 6), -BLK_DEV, 2 * BLK_DEV, dtype=jnp.int32)
    offset = offset.at[0, 0].set(-1)
    target = jnp.mod(rows - jnp.mod(rows, BLK_DEV) + offset, BLOCKS)
    opened = jax.random.randint(key_open, (BLOCKS, 6), 0, 6, dtype=jnp.int32) == 0
    opened = opened.at[0, 0].set(False)
    opened = opened.at[BLOCKS - 1, 5].set(True)
    return jnp.where(opened, -1, target).astype(jnp.int32)


def with_ends(values, rng, smallest, top_value):
    dims = values.shape
    spot = [jax.random.randint(jax.random.fold_in(rng, axis), (), 0, dims[axis]) for axis in range(len(dims))]
    values = values.at[tuple(spot)].set(smallest)
    longest = dims.index(max(dims))
    spot[longest] = (spot[longest] + 1) % dims[longest]
    return values.at[tuple(spot)].set(top_value)


def steps_of(own_key, extent, shards, low, largest):
    def one(axis_at, blocks):
        draws = jax.random.uniform(jax.random.fold_in(jax.random.fold_in(own_key, 6), axis_at), (blocks,), jnp.float32, low / len(shards), largest / len(shards))
        return jnp.repeat(jnp.exp(draws), extent[axis_at] // blocks).reshape((-1,) + (1,) * (len(extent) - axis_at - 1))

    factor_of = one(*shards[0])
    for cut in shards[1:]:
        factor_of = factor_of * one(*cut)
    return factor_of


def setup_inputs(seed: int = 0) -> dict:
    arg_keys = jax.random.split(jax.random.key(seed), 4)
    dist = jnp.clip(jnp.exp(math.log(10.0) - 4.6051702 * jax.random.uniform(arg_keys[0], (BLOCKS, CELLS, NV), jnp.float32) ** steps_of(arg_keys[0], (BLOCKS, CELLS, NV), ((0, 64), (2, 16)), -0.2, 0.2)), 0.1, 10.0)
    neighbours = draw_neighbours(jax.random.fold_in(arg_keys[3], 71), 0)
    solid = with_ends((jax.random.randint(arg_keys[2], (BLOCKS, CELLS), 0, 6) < 1).astype(jnp.int32), jax.random.fold_in(arg_keys[2], 1), 0, 1)
    return {"dist": dist, "neighbours": neighbours, "solid": solid}


velocity_step = 0.5
diffusivity_ratio = 2.0 / 3.0
viscosity_exponent = 0.19
rarefaction_ratio = 100.0
courant = 0.9


def timestep_length():
    return courant / (1.5 * (NVX - 1) * velocity_step)


def velocity_grid(first_index, local_count):
    indices = first_index + jnp.arange(local_count, dtype=jnp.int32)
    along_x = indices // (NVX * NVX)
    along_y = (indices // NVX) % NVX
    along_z = indices % NVX
    centre = (NVX - 1) / 2.0
    return tuple((axis_index.astype(jnp.float32) - centre) * velocity_step for axis_index in (along_x, along_y, along_z))


def gaussian_population(molecule_concentration, bulk_flow_first, bulk_flow_second, bulk_flow_third, kinetic_heat_level, molecule_motion_grid):
    random_motion_width = (molecule_motion_grid[0] - bulk_flow_first) ** 2 + (molecule_motion_grid[1] - bulk_flow_second) ** 2 + (molecule_motion_grid[2] - bulk_flow_third) ** 2
    return molecule_concentration * (2.0 * math.pi * kinetic_heat_level) ** -1.5 * jnp.exp(-random_motion_width / (2.0 * kinetic_heat_level))


def boundary_layers(volume):
    leading = volume.shape[0]
    trailing = volume.shape[-1]
    pieces = [volume[:, 0], volume[:, -1], volume[:, :, 0], volume[:, :, -1], volume[:, :, :, 0], volume[:, :, :, -1]]
    return jnp.stack([piece.reshape(leading, BS * BS, trailing) for piece in pieces], axis=1)


def transport(volume, ghosts, molecule_motion_grid):
    leading = volume.shape[0]
    trailing = volume.shape[-1]
    shaped = ghosts.reshape(leading, 6, BS, BS, trailing)
    behind_x = jnp.concatenate([shaped[:, 0][:, None], volume[:, :-1]], axis=1)
    ahead_x = jnp.concatenate([volume[:, 1:], shaped[:, 1][:, None]], axis=1)
    behind_y = jnp.concatenate([shaped[:, 2][:, :, None], volume[:, :, :-1]], axis=2)
    ahead_y = jnp.concatenate([volume[:, :, 1:], shaped[:, 3][:, :, None]], axis=2)
    behind_z = jnp.concatenate([shaped[:, 4][:, :, :, None], volume[:, :, :, :-1]], axis=3)
    ahead_z = jnp.concatenate([volume[:, :, :, 1:], shaped[:, 5][:, :, :, None]], axis=3)
    upwind = jnp.maximum(molecule_motion_grid[0], 0.0) * (volume - behind_x) + jnp.minimum(molecule_motion_grid[0], 0.0) * (ahead_x - volume)
    upwind = upwind + jnp.maximum(molecule_motion_grid[1], 0.0) * (volume - behind_y) + jnp.minimum(molecule_motion_grid[1], 0.0) * (ahead_y - volume)
    upwind = upwind + jnp.maximum(molecule_motion_grid[2], 0.0) * (volume - behind_z) + jnp.minimum(molecule_motion_grid[2], 0.0) * (ahead_z - volume)
    return volume - timestep_length() * upwind


def primary_integrals(grid_site_values, molecule_motion_grid):
    weight = velocity_step ** 3
    unity = jnp.ones_like(molecule_motion_grid[0])
    second_power = molecule_motion_grid[0] ** 2 + molecule_motion_grid[1] ** 2 + molecule_motion_grid[2] ** 2
    weights_table = jnp.stack([unity, molecule_motion_grid[0], molecule_motion_grid[1], molecule_motion_grid[2], second_power]) * weight
    return lax.dot_general(weights_table, grid_site_values, (((1,), (1,)), ((), ())), precision=lax.Precision.HIGHEST, preferred_element_type=jnp.float32)


def hydrodynamic_quantities(primary_totals):
    molecule_concentration = primary_totals[0]
    bulk_flow_vector = primary_totals[1:4] / molecule_concentration
    kinetic_heat_level = (primary_totals[4] / molecule_concentration - jnp.sum(bulk_flow_vector * bulk_flow_vector, axis=0)) / 3.0
    return molecule_concentration, bulk_flow_vector, kinetic_heat_level


def heat_terms(grid_site_values, molecule_motion_grid, bulk_flow_vector):
    weight = velocity_step ** 3
    relative = [molecule_motion_grid[axis_number][None, :] - bulk_flow_vector[axis_number][:, None] for axis_number in range(3)]
    second_power = relative[0] ** 2 + relative[1] ** 2 + relative[2] ** 2
    return jnp.stack([jnp.sum(part * second_power * grid_site_values, axis=1) for part in relative]) * weight


def collision_correction(grid_site_values, molecule_concentration, bulk_flow_vector, kinetic_heat_level, interface_transfers, molecule_motion_grid):
    relative = [molecule_motion_grid[axis_number][None, :] - bulk_flow_vector[axis_number][:, None] for axis_number in range(3)]
    second_power = relative[0] ** 2 + relative[1] ** 2 + relative[2] ** 2
    mass_per_volume_vector = molecule_concentration[:, None]
    heat_level_vector = kinetic_heat_level[:, None]
    target_population = mass_per_volume_vector * (2.0 * math.pi * heat_level_vector) ** -1.5 * jnp.exp(-second_power / (2.0 * heat_level_vector))
    normal_stress = mass_per_volume_vector * heat_level_vector
    subspace_mapping = relative[0] * interface_transfers[0][:, None] + relative[1] * interface_transfers[1][:, None] + relative[2] * interface_transfers[2][:, None]
    heat_corrected_model = target_population * (1.0 + (1.0 - diffusivity_ratio) * subspace_mapping / (5.0 * normal_stress * heat_level_vector) * (second_power / heat_level_vector - 5.0))
    collision_frequency = timestep_length() * mass_per_volume_vector * heat_level_vector ** viscosity_exponent / rarefaction_ratio
    return (grid_site_values + collision_frequency * heat_corrected_model) / (1.0 + collision_frequency)


def reference(dist, neighbours, solid):
    molecule_motion_grid = velocity_grid(0, NV)
    wall_state = gaussian_population(20.0, 0.0, 0.0, 0.0, 2.0, molecule_motion_grid)
    inflow = gaussian_population(20.0, 2.5, 0.0, 0.0, 1.0, molecule_motion_grid)
    opposite = jnp.array([1, 0, 3, 2, 5, 4], dtype=jnp.int32)
    wall_faces = boundary_layers(solid.reshape(BLOCKS, BS, BS, BS, 1)) == 1
    present_dist = dist
    for repeat in range(ITERS):
        layers = jnp.where(wall_faces, wall_state, boundary_layers(present_dist.reshape(BLOCKS, BS, BS, BS, NV)))

        def advance(member):
            block_field, block_solid, block_links = member
            filled = jnp.where(block_solid[:, None] == 1, wall_state, block_field)
            clipped = jnp.maximum(block_links, 0).astype(jnp.int32)
            ghosts = layers[clipped, opposite]
            ghosts = jnp.where(block_links[:, None, None] < 0, inflow, ghosts)
            advected_population = transport(filled.reshape(1, BS, BS, BS, NV), ghosts[None], molecule_motion_grid).reshape(CELLS, NV)
            molecule_concentration, bulk_flow_vector, kinetic_heat_level = hydrodynamic_quantities(primary_integrals(advected_population, molecule_motion_grid))
            interface_transfers = heat_terms(advected_population, molecule_motion_grid, bulk_flow_vector)
            return collision_correction(advected_population, molecule_concentration, bulk_flow_vector, kinetic_heat_level, interface_transfers, molecule_motion_grid)

        present_dist = lax.map(advance, (present_dist, solid, neighbours))
    return jnp.where(solid[:, :, None] == 1, wall_state, present_dist)
```

```python
import math

import jax
import jax.numpy as jnp
from jax import lax
from jax.experimental import pallas as pl
from jax.experimental.pallas import tpu as pltpu
from jax.sharding import PartitionSpec as P

NVX = 16
BS = 8
ITERS = 2
CELLS = BS * BS * BS
GROUPS = BS * BS
LANES = NVX * NVX
HALF = LANES // 2

velocity_step = 0.5
diffusivity_ratio = 2.0 / 3.0
viscosity_exponent = 0.19
rarefaction_ratio = 100.0
courant = 0.9
dt = courant / (1.5 * (NVX - 1) * velocity_step)
weight = velocity_step**3
centre = (NVX - 1) / 2.0

F32 = jnp.float32


def lane_velocities(rows=1):
    lane = lax.broadcasted_iota(jnp.int32, (rows, LANES), 1)
    cy = ((lane >> 4).astype(F32) - centre) * velocity_step
    cz = ((lane & (NVX - 1)).astype(F32) - centre) * velocity_step
    return cy, cz


def own_cx():
    return (lax.axis_index("vel").astype(F32) - centre) * velocity_step


def maxwellian(rho, ux, temperature, cx, cy, cz):
    width = (cx - ux) * (cx - ux) + cy * cy + cz * cz
    return rho * (2.0 * math.pi * temperature) ** (-1.5) * jnp.exp(width * (-0.5 / temperature))


def store_faces(filled, faces):
    _, cz = lane_velocities(GROUPS)
    positive = lax.axis_index("vel") >= NVX // 2
    first = pl.multiple_of(jnp.where(positive, (BS - 1) * GROUPS, 0), GROUPS)
    for half in range(2):
        faces[half, 0] = filled[half, pl.ds(first, GROUPS), :]
        for i in range(BS):
            row = i * GROUPS + half * (BS - 1) * BS
            faces[half, 1, i * BS : (i + 1) * BS, :] = filled[half, row : row + BS, :]
        bottom = filled[half, pl.ds(0, GROUPS, stride=BS), :]
        top = filled[half, pl.ds(BS - 1, GROUPS, stride=BS), :]
        upward = cz[:, half * HALF : (half + 1) * HALF] > 0
        faces[half, 2] = jnp.where(upward, top, bottom)


def fill_kernel(dist, solid, filled, faces):
    cx = own_cx()
    cy, cz = lane_velocities()
    wall = maxwellian(20.0, 0.0, 2.0, cx, cy, cz)
    flags = jnp.broadcast_to(solid[...].astype(F32), (BS, CELLS))
    top = lax.broadcasted_iota(jnp.int32, (BS, HALF), 0) == 0
    mask = lax.dot_general(
        flags, top.astype(F32), (((0,), (0,)), ((), ())), preferred_element_type=F32
    )
    inside = mask > 0.5
    for half in range(2):
        lanes = slice(half * HALF, (half + 1) * HALF)
        filled[half] = jnp.where(inside, wall[:, lanes], dist[:, lanes])
    store_faces(filled, faces)


def advect_kernel(neighbours, filled, own, below, above, advected, partial, ghost_z):
    cx = own_cx()
    cy, cz = lane_velocities()
    here = lax.axis_index("space")
    count = lax.axis_size("space")
    inflow = maxwellian(20.0, 2.5, 1.0, cx, cy, cz)

    def pick(face, dim, half):
        block = neighbours[0, face]
        place = lax.rem(block - here + 1 + count, count)
        value = jnp.where(place == 0, below[half, dim], above[half, dim])
        value = jnp.where(place == 1, own[half, dim], value)
        return jnp.where(block < 0, inflow[:, half * HALF : (half + 1) * HALF], value)

    positive = lax.axis_index("vel") >= NVX // 2
    face_x = jnp.where(positive, 0, 1)
    kx = dt * jnp.abs(cx)
    ky = dt * jnp.abs(cy)
    kz = dt * jnp.abs(cz)
    keep = 1.0 - kx - ky - kz
    sub = lax.broadcasted_iota(jnp.int32, (BS, HALF), 0)
    row_weights = []
    for half in range(2):
        lanes = slice(half * HALF, (half + 1) * HALF)
        upward = jnp.broadcast_to(cz[:, lanes] > 0, (BS, HALF))
        edge = (sub == 0) & upward | (sub == BS - 1) & jnp.logical_not(upward)
        gx = pick(face_x, 0, half)
        gy = pick(3 if half == 0 else 2, 1, half)
        up64 = jnp.broadcast_to(cz[:, lanes] > 0, (GROUPS, HALF))
        ghost_z[half] = jnp.where(up64, pick(4, 2, half), pick(5, 2, half))
        k0 = jnp.broadcast_to(keep[:, lanes], (BS, HALF))
        k2 = jnp.broadcast_to(ky[:, lanes], (BS, HALF))
        k3 = jnp.broadcast_to(kz[:, lanes], (BS, HALF))
        for i in range(BS):
            for j in range(BS):
                row = (i * BS + j) * BS
                value = filled[half, row : row + BS]
                down_row = max(row - GROUPS, 0)
                up_row = min(row + GROUPS, CELLS - BS)
                x_low = filled[half, down_row : down_row + BS]
                x_high = filled[half, up_row : up_row + BS]
                if i == 0:
                    x_low = gx[j * BS : (j + 1) * BS]
                if i == BS - 1:
                    x_high = gx[j * BS : (j + 1) * BS]
                x_up = jnp.where(positive, x_low, x_high)
                if half == 0:
                    y_up = (
                        filled[half, row + BS : row + 2 * BS]
                        if j < BS - 1
                        else gy[i * BS : (i + 1) * BS]
                    )
                else:
                    y_up = (
                        filled[half, row - BS : row] if j > 0 else gy[i * BS : (i + 1) * BS]
                    )
                group = i * BS + j
                z_up = jnp.where(upward, pltpu.roll(value, 1, 0), pltpu.roll(value, BS - 1, 0))
                z_ghost = jnp.broadcast_to(ghost_z[half, group : group + 1], (BS, HALF))
                z_up = jnp.where(edge, z_ghost, z_up)
                advected[half, row : row + BS] = k0 * value + kx * x_up + k2 * y_up + k3 * z_up
    one = jnp.ones_like(cy)
    plane = cy * cy + cz * cz
    table = jnp.concatenate(
        [one, cy, cz, cy * cy, cz * cz, cy * cz, cy * plane, cz * plane], axis=0
    )
    total = None
    for half in range(2):
        term = lax.dot_general(
            table[:, half * HALF : (half + 1) * HALF] * weight,
            advected[half],
            (((1,), (1,)), ((), ())),
            precision=lax.Precision.HIGHEST,
            preferred_element_type=F32,
        )
        total = term if total is None else total + term
    partial[...] = total


def collide_kernel(gathered, solid, advected, out, faces, turned):
    sums = [jnp.zeros((BS, CELLS), F32) for _ in range(4)]
    for a in range(NVX):
        ca = (a - centre) * velocity_step
        part = gathered[a]
        for n in range(4):
            sums[n] = sums[n] + part * ca**n

    def row(n, r):
        return sums[n][r : r + 1, :]

    rho = row(0, 0)
    jx, jy, jz = row(1, 0), row(0, 1), row(0, 2)
    pxx, pyy, pzz = row(2, 0), row(0, 3), row(0, 4)
    pxy, pxz, pyz = row(1, 1), row(1, 2), row(0, 5)
    hx = row(3, 0) + row(1, 3) + row(1, 4)
    hy = row(2, 1) + row(0, 6)
    hz = row(2, 2) + row(0, 7)
    energy = pxx + pyy + pzz
    ux, uy, uz = jx / rho, jy / rho, jz / rho
    speed = ux * ux + uy * uy + uz * uz
    temperature = (energy / rho - speed) / 3.0
    twice = 2.0 * rho * speed
    qx = hx - 2.0 * (ux * pxx + uy * pxy + uz * pxz) - ux * energy + ux * twice
    qy = hy - 2.0 * (ux * pxy + uy * pyy + uz * pyz) - uy * energy + uy * twice
    qz = hz - 2.0 * (ux * pxz + uy * pyz + uz * pzz) - uz * energy + uz * twice
    log_t = jnp.log(temperature)
    rate = (dt / rarefaction_ratio) * rho * jnp.exp(viscosity_exponent * log_t)
    keep = 1.0 / (1.0 + rate)
    amount = rate * keep * rho * (2.0 * math.pi) ** (-1.5) * jnp.exp(-1.5 * log_t)
    scale = ((1.0 - diffusivity_ratio) / 5.0) / (rho * temperature * temperature)
    cx = own_cx()
    rx = cx - ux
    inside = solid[...] == 1
    zero = jnp.zeros_like(rho)
    wall_amount = 20.0 * (2.0 * math.pi * 2.0) ** (-1.5)
    rows = [
        jnp.where(inside, zero, uy),
        jnp.where(inside, zero, uz),
        jnp.where(inside, cx * cx, rx * rx),
        jnp.where(inside, zero, qy * scale),
        jnp.where(inside, zero, qz * scale),
        jnp.where(inside, zero, rx * qx * scale),
        jnp.where(inside, -0.25, -0.5 / temperature),
        jnp.where(inside, wall_amount, amount),
        jnp.where(inside, zero, keep),
    ]
    rows = rows + [zero] * (NVX - len(rows))
    turned[...] = jnp.concatenate(rows, axis=0).T
    cy, cz = lane_velocities(BS)
    for group in range(GROUPS):
        at = slice(group * BS, (group + 1) * BS)
        cell = turned[at, :]

        def wide(k):
            return jnp.broadcast_to(cell[:, k : k + 1], (BS, HALF))

        vy, vz, rx2, sy, sz, sx, slope, top, stay = [wide(k) for k in range(9)]
        for half in range(2):
            lanes = slice(half * HALF, (half + 1) * HALF)
            ry = cy[:, lanes] - vy
            rz = cz[:, lanes] - vz
            exponent = (ry * ry + rz * rz + rx2) * slope
            flow = ry * sy + rz * sz + sx
            shape = 1.0 + flow * (-2.0 * exponent - 5.0)
            value = stay * advected[half, at] + top * jnp.exp(exponent) * shape
            if faces is None:
                out[at, lanes] = value
            else:
                out[half, at] = value
    if faces is not None:
        store_faces(out, faces)


def last_kernel(gathered, solid, advected, out, turned):
    collide_kernel(gathered, solid, advected, out, None, turned)


VMEM = pl.BlockSpec(memory_space=pltpu.VMEM)
SMEM = pl.BlockSpec(memory_space=pltpu.SMEM)
FIELD = jax.ShapeDtypeStruct((2, CELLS, HALF), F32)
RESULT = jax.ShapeDtypeStruct((CELLS, LANES), F32)
FACES = jax.ShapeDtypeStruct((2, 3, GROUPS, HALF), F32)
PARTIAL = jax.ShapeDtypeStruct((BS, CELLS), F32)


def call(kernel, ins, outs, scratch=()):
    return pl.pallas_call(
        kernel,
        in_specs=ins,
        out_specs=[VMEM] * len(outs),
        out_shape=outs,
        scratch_shapes=list(scratch),
        compiler_params=pltpu.CompilerParams(vmem_limit_bytes=16 * 1024 * 1024),
    )


def on_device(dist, neighbours, solid):
    count = lax.axis_size("space")
    forward = [(i, (i + 1) % count) for i in range(count)]
    backward = [(target, source) for source, target in forward]
    filled, faces = call(fill_kernel, [VMEM] * 2, [FIELD, FACES])(dist[0], solid)
    for step in range(ITERS):
        below = lax.ppermute(faces, "space", forward)
        above = lax.ppermute(faces, "space", backward)
        advected, partial = call(
            advect_kernel,
            [SMEM] + [VMEM] * 4,
            [FIELD, PARTIAL],
            [pltpu.VMEM((2, GROUPS, HALF), F32)],
        )(neighbours, filled, faces, below, above)
        copies = jnp.broadcast_to(partial, (NVX, BS, CELLS))
        gathered = lax.all_to_all(copies, "vel", 0, 0, tiled=True)
        turned = [pltpu.VMEM((CELLS, NVX), F32)]
        if step < ITERS - 1:
            filled, faces = call(collide_kernel, [VMEM] * 3, [FIELD, FACES], turned)(
                gathered, solid, advected
            )
        else:
            (filled,) = call(last_kernel, [VMEM] * 3, [RESULT], turned)(gathered, solid, advected)
    return filled[None]


def solution(mesh):
    in_specs = (P("space", None, "vel"), P("space", None), P("space", None))
    out_specs = P("space", None, "vel")
    return jax.shard_map(
        on_device, mesh=mesh, in_specs=in_specs, out_specs=out_specs, check_vma=False
    )
```

```python
import math

import jax
import jax.numpy as jnp
from jax import lax
from jax.experimental import pallas as pl
from jax.experimental.pallas import tpu as pltpu
from jax.sharding import PartitionSpec as P


NVX = 16
BS = 8
ITERS = 2
CELLS = BS * BS * BS
GROUPS = BS * BS
LANES = NVX * NVX
HALF = LANES // 2

velocity_step = 0.5
diffusivity_ratio = 2.0 / 3.0
viscosity_exponent = 0.19
rarefaction_ratio = 100.0
courant = 0.9
dt = courant / (1.5 * (NVX - 1) * velocity_step)
weight = velocity_step**3
centre = (NVX - 1) / 2.0

F32 = jnp.float32


def lane_velocities(rows=1):
    lane = lax.broadcasted_iota(jnp.int32, (rows, LANES), 1)
    cy = ((lane >> 4).astype(F32) - centre) * velocity_step
    cz = ((lane & (NVX - 1)).astype(F32) - centre) * velocity_step
    return cy, cz


def own_cx():
    return (lax.axis_index("vel").astype(F32) - centre) * velocity_step


def maxwellian(rho, ux, temperature, cx, cy, cz):
    width = (cx - ux) * (cx - ux) + cy * cy + cz * cz
    return rho * (2.0 * math.pi * temperature) ** (-1.5) * jnp.exp(width * (-0.5 / temperature))


def store_faces(filled, faces):
    _, cz = lane_velocities(GROUPS)
    positive = lax.axis_index("vel") >= NVX // 2
    first = pl.multiple_of(jnp.where(positive, (BS - 1) * GROUPS, 0), GROUPS)
    for half in range(2):
        faces[half, 0] = filled[half, pl.ds(first, GROUPS), :]
        for i in range(BS):
            row = i * GROUPS + half * (BS - 1) * BS
            faces[half, 1, i * BS : (i + 1) * BS, :] = filled[half, row : row + BS, :]
        bottom = filled[half, pl.ds(0, GROUPS, stride=BS), :]
        top = filled[half, pl.ds(BS - 1, GROUPS, stride=BS), :]
        upward = cz[:, half * HALF : (half + 1) * HALF] > 0
        faces[half, 2] = jnp.where(upward, top, bottom)


def fill_kernel(dist_hbm, solid_hbm, filled, faces, dist, solid, sems):
    copies = [
        pltpu.make_async_copy(solid_hbm, solid, sems.at[0]),
        pltpu.make_async_copy(dist_hbm, dist, sems.at[1]),
    ]
    for copy in copies:
        copy.start()
    cx = own_cx()
    cy, cz = lane_velocities()
    wall = maxwellian(20.0, 0.0, 2.0, cx, cy, cz)
    top = lax.broadcasted_iota(jnp.int32, (BS, HALF), 0) == 0
    copies[0].wait()
    flags = jnp.broadcast_to(solid[...].astype(F32), (BS, CELLS))
    mask = lax.dot_general(
        flags, top.astype(F32), (((0,), (0,)), ((), ())), preferred_element_type=F32
    )
    inside = mask > 0.5
    copies[1].wait()
    for half in range(2):
        lanes = slice(half * HALF, (half + 1) * HALF)
        filled[half] = jnp.where(inside, wall[:, lanes], dist[:, lanes])
    store_faces(filled, faces)


def upwind_edge(cz, sub):
    upward = jnp.broadcast_to(cz > 0, (BS, HALF))
    return upward, (sub == 0) & upward | (sub == BS - 1) & jnp.logical_not(upward)


def inner_kernel(filled, inner):
    cx = own_cx()
    cy, cz = lane_velocities()
    positive = lax.axis_index("vel") >= NVX // 2
    kx = dt * jnp.abs(cx)
    ky = dt * jnp.abs(cy)
    kz = dt * jnp.abs(cz)
    keep = 1.0 - kx - ky - kz
    sub = lax.broadcasted_iota(jnp.int32, (BS, HALF), 0)
    for half in range(2):
        lanes = slice(half * HALF, (half + 1) * HALF)
        upward, edge = upwind_edge(cz[:, lanes], sub)
        k0 = jnp.broadcast_to(keep[:, lanes], (BS, HALF))
        k2 = jnp.broadcast_to(ky[:, lanes], (BS, HALF))
        k3 = jnp.where(edge, 0.0, jnp.broadcast_to(kz[:, lanes], (BS, HALF)))
        low_x = jnp.where(positive, kx, 0.0)
        high_x = jnp.where(positive, 0.0, kx)
        for i in range(BS):
            for j in range(BS):
                row = (i * BS + j) * BS
                value = filled[half, row : row + BS]
                total = k0 * value
                if i > 0:
                    total = total + low_x * filled[half, row - GROUPS : row - GROUPS + BS]
                if i < BS - 1:
                    total = total + high_x * filled[half, row + GROUPS : row + GROUPS + BS]
                if half == 0 and j < BS - 1:
                    total = total + k2 * filled[half, row + BS : row + 2 * BS]
                if half == 1 and j > 0:
                    total = total + k2 * filled[half, row - BS : row]
                z_up = jnp.where(upward, pltpu.roll(value, 1, 0), pltpu.roll(value, BS - 1, 0))
                inner[half, row : row + BS] = total + k3 * z_up


def ghost_kernel(neighbours, inner, own, below, above, advected, partial, ghost_z):
    cx = own_cx()
    cy, cz = lane_velocities()
    here = lax.axis_index("space")
    count = lax.axis_size("space")
    inflow = maxwellian(20.0, 2.5, 1.0, cx, cy, cz)

    block = neighbours[...]
    places = jnp.where(block < 0, 3, lax.rem(block - here + 1 + count, count))

    def pick(place, dim, half):
        place = jnp.broadcast_to(place, (GROUPS, HALF))
        value = jnp.where(place == 0, below[half, dim], above[half, dim])
        value = jnp.where(place == 1, own[half, dim], value)
        return jnp.where(place == 3, inflow[:, half * HALF : (half + 1) * HALF], value)

    positive = lax.axis_index("vel") >= NVX // 2
    face = [places[:, k : k + 1] for k in range(6)]
    face_x = jnp.where(positive, face[0], face[1])
    first = pl.multiple_of(jnp.where(positive, 0, (BS - 1) * GROUPS), GROUPS)
    kx = dt * jnp.abs(cx)
    ky = dt * jnp.abs(cy)
    kz = dt * jnp.abs(cz)
    sub = lax.broadcasted_iota(jnp.int32, (BS, HALF), 0)
    one = jnp.ones_like(cy)
    plane = cy * cy + cz * cz
    table = weight * jnp.concatenate(
        [one, cy, cz, cy * cy, cz * cz, cy * cz, cy * plane, cz * plane], axis=0
    )
    coarse = table.astype(jnp.bfloat16)
    table = jnp.concatenate([coarse.astype(F32), table - coarse.astype(F32)], axis=0)
    table = table.astype(jnp.bfloat16)
    total = jnp.zeros((2 * BS, CELLS), F32)
    for half in range(2):
        lanes = slice(half * HALF, (half + 1) * HALF)
        _, edge = upwind_edge(cz[:, lanes], sub)
        side = edge.astype(F32)
        up64 = jnp.broadcast_to(cz[:, lanes] > 0, (GROUPS, HALF))
        ghost_z[half] = kz[:, lanes] * jnp.where(up64, pick(face[4], 2, half), pick(face[5], 2, half))
        gy = ky[:, lanes] * pick(face[3 - half], 1, half)
        gx = kx * pick(face_x, 0, half)
        for i in range(BS):
            for j in range(BS):
                group = i * BS + j
                at = slice(group * BS, (group + 1) * BS)
                z_ghost = jnp.broadcast_to(ghost_z[half, group : group + 1], (BS, HALF))
                value = inner[half, at] + side * z_ghost
                if j == (BS - 1 if half == 0 else 0):
                    value = value + gy[i * BS : (i + 1) * BS]
                advected[half, at] = value
        rows = pl.ds(first, GROUPS)
        advected[half, rows] = advected[half, rows] + gx
        value = advected[half]
        high = value.astype(jnp.bfloat16)
        low = (value - high.astype(F32)).astype(jnp.bfloat16)
        for piece in (high, low):
            total = total + lax.dot_general(
                table[:, lanes],
                piece,
                (((1,), (1,)), ((), ())),
                preferred_element_type=F32,
            )
    partial[...] = total[:BS] + total[BS:]


def bfloat_pieces(value):
    pieces = []
    for _ in range(3):
        piece = value.astype(jnp.bfloat16).astype(F32)
        pieces.append(piece)
        value = value - piece
    return pieces


def cell_basis():
    cy, cz = lane_velocities(NVX)
    row = lax.broadcasted_iota(jnp.int32, (NVX, LANES), 0)
    zero = jnp.zeros((NVX, LANES), F32)

    def rows(first, entries):
        out = zero
        for k, entry in enumerate(entries):
            out = jnp.where(row == first + k, entry, out)
        return out

    exponent = rows(0, [cy * cy + cz * cz, cy, cz, 1.0])
    flow = rows(4, [cy, cz, 1.0])
    stay = rows(7, [1.0])[:, :HALF]
    top = rows(8, [1.0])[:, :HALF]
    block = jnp.concatenate([exponent, flow, stay, top], axis=1)
    return jnp.concatenate([block] * 3, axis=0).astype(jnp.bfloat16)


def collide(gathered, solid, advected, turned, store):
    sums = [None] * 4
    for a in range(NVX // 2, NVX):
        ca = (a - centre) * velocity_step
        high, low = gathered[a], gathered[NVX - 1 - a]
        even, odd = high + low, high - low
        terms = [even, ca * odd, ca**2 * even, ca**3 * odd]
        sums = [t if s is None else s + t for s, t in zip(sums, terms)]

    def row(n, r):
        return sums[n][r : r + 1, :]

    rho = row(0, 0)
    jx, jy, jz = row(1, 0), row(0, 1), row(0, 2)
    pxx, pyy, pzz = row(2, 0), row(0, 3), row(0, 4)
    pxy, pxz, pyz = row(1, 1), row(1, 2), row(0, 5)
    hx = row(3, 0) + row(1, 3) + row(1, 4)
    hy = row(2, 1) + row(0, 6)
    hz = row(2, 2) + row(0, 7)
    energy = pxx + pyy + pzz
    inverse = 1.0 / rho
    ux, uy, uz = jx * inverse, jy * inverse, jz * inverse
    speed = ux * ux + uy * uy + uz * uz
    temperature = (energy * inverse - speed) / 3.0
    twice = 2.0 * rho * speed - energy
    qx = hx - 2.0 * (ux * pxx + uy * pxy + uz * pxz) + ux * twice
    qy = hy - 2.0 * (ux * pxy + uy * pyy + uz * pyz) + uy * twice
    qz = hz - 2.0 * (ux * pxz + uy * pyz + uz * pzz) + uz * twice
    log_t = jnp.log(temperature)
    cold = 1.0 / temperature
    rate = (dt / rarefaction_ratio) * rho * jnp.exp(viscosity_exponent * log_t)
    keep = 1.0 / (1.0 + rate)
    amount = rate * keep * rho * (2.0 * math.pi) ** (-1.5) * jnp.exp(-1.5 * log_t)
    scale = ((1.0 - diffusivity_ratio) / 5.0) * inverse * cold * cold
    cx = own_cx()
    rx = cx - ux
    slope = -0.5 * cold
    sy, sz = qy * scale, qz * scale
    inside = solid[...] == 1
    wall_amount = 20.0 * (2.0 * math.pi * 2.0) ** (-1.5)
    rows = [
        jnp.where(inside, -0.25, slope),
        jnp.where(inside, 0.0, cold * uy),
        jnp.where(inside, 0.0, cold * uz),
        jnp.where(inside, -0.25 * (cx * cx), slope * (rx * rx + uy * uy + uz * uz)),
        jnp.where(inside, 0.0, sy),
        jnp.where(inside, 0.0, sz),
        jnp.where(inside, 0.0, rx * qx * scale - sy * uy - sz * uz),
        jnp.where(inside, 0.0, keep),
        jnp.where(inside, wall_amount, amount),
    ]
    rows = rows + [jnp.zeros_like(rho)] * (NVX - len(rows))
    pieces = jnp.concatenate(bfloat_pieces(jnp.concatenate(rows, axis=0)), axis=0)
    turned[...] = pieces.T.astype(jnp.bfloat16)
    basis = cell_basis()
    chunk = 2 * GROUPS
    for first in range(0, CELLS, chunk):
        at = slice(first, first + chunk)
        wide = jnp.dot(turned[at], basis, preferred_element_type=F32)
        stay = wide[:, 2 * LANES : 2 * LANES + HALF]
        top = wide[:, 2 * LANES + HALF :]
        for half in range(2):
            exponent = wide[:, half * HALF : (half + 1) * HALF]
            flow = wide[:, LANES + half * HALF : LANES + (half + 1) * HALF]
            shape = 1.0 + flow * (-2.0 * exponent - 5.0)
            value = stay * advected[half, at] + top * jnp.exp(exponent) * shape
            store(half, first, chunk, value)


def collide_kernel(gathered, solid, advected, filled, faces, turned):
    def store(half, first, count, value):
        filled[half, first : first + count] = value

    collide(gathered, solid, advected, turned, store)
    store_faces(filled, faces)


def last_kernel(gathered, solid, advected, result, turned, out, sems):
    copies = []

    def store(half, first, count, value):
        out[first : first + count, half * HALF : (half + 1) * HALF] = value
        if half == 1:
            at = pl.ds(first, count)
            copy = pltpu.make_async_copy(out.at[at], result.at[at], sems.at[len(copies)])
            copy.start()
            copies.append(copy)

    collide(gathered, solid, advected, turned, store)
    for copy in copies:
        copy.wait()


VMEM = pl.BlockSpec(memory_space=pltpu.VMEM)
HBM = pl.BlockSpec(memory_space=pltpu.HBM)
FIELD = jax.ShapeDtypeStruct((2, CELLS, HALF), F32)
RESULT = jax.ShapeDtypeStruct((CELLS, LANES), F32)
FACES = jax.ShapeDtypeStruct((2, 3, GROUPS, HALF), F32)
PARTIAL = jax.ShapeDtypeStruct((BS, CELLS), F32)
TURNED = pltpu.VMEM((CELLS, 3 * NVX), jnp.bfloat16)


def call(kernel, ins, outs, scratch=(), out_spec=VMEM):
    size = CELLS * LANES
    return pl.pallas_call(
        kernel,
        in_specs=ins,
        out_specs=[out_spec] * len(outs),
        out_shape=outs,
        scratch_shapes=list(scratch),
        cost_estimate=pl.CostEstimate(
            flops=40 * size, transcendentals=size, bytes_accessed=8 * size
        ),
        compiler_params=pltpu.CompilerParams(vmem_limit_bytes=16 * 1024 * 1024),
    )


def on_device(dist, neighbours, solid):
    count = lax.axis_size("space")
    forward = [(i, (i + 1) % count) for i in range(count)]
    backward = [(target, source) for source, target in forward]
    filled, faces = call(
        fill_kernel,
        [HBM] * 2,
        [FIELD, FACES],
        [
            pltpu.VMEM((CELLS, LANES), F32),
            pltpu.VMEM((1, CELLS), jnp.int32),
            pltpu.SemaphoreType.DMA((2,)),
        ],
    )(
        pltpu.with_memory_space_constraint(dist[0], pltpu.HBM),
        pltpu.with_memory_space_constraint(solid, pltpu.HBM),
    )
    for step in range(ITERS):
        below = lax.ppermute(faces, "space", forward)
        above = lax.ppermute(faces, "space", backward)
        (inner,) = call(inner_kernel, [VMEM], [FIELD])(filled)
        advected, partial = call(
            ghost_kernel,
            [VMEM] * 5,
            [FIELD, PARTIAL],
            [pltpu.VMEM((2, GROUPS, HALF), F32)],
        )(neighbours, inner, faces, below, above)
        copies = jnp.broadcast_to(partial, (NVX, BS, CELLS))
        gathered = lax.all_to_all(copies, "vel", 0, 0, tiled=True)
        if step < ITERS - 1:
            filled, faces = call(collide_kernel, [VMEM] * 3, [FIELD, FACES], [TURNED])(
                gathered, solid, advected
            )
        else:
            (filled,) = call(
                last_kernel,
                [VMEM] * 3,
                [RESULT],
                [TURNED, pltpu.VMEM((CELLS, LANES), F32), pltpu.SemaphoreType.DMA((4,))],
                HBM,
            )(gathered, solid, advected)
    return filled[None]


def solution(mesh):
    in_specs = (P("space", None, "vel"), P("space", None), P("space", None))
    out_specs = P("space", None, "vel")
    return jax.shard_map(
        on_device, mesh=mesh, in_specs=in_specs, out_specs=out_specs, check_vma=False
    )
```

```python
import math

import jax
import jax.numpy as jnp
from jax import lax
from jax.experimental import pallas as pl
from jax.experimental.pallas import tpu as pltpu
from jax.sharding import PartitionSpec as P


NVX = 16
BS = 8
ITERS = 2
CELLS = BS * BS * BS
GROUPS = BS * BS
LANES = NVX * NVX
HALF = LANES // 2

velocity_step = 0.5
diffusivity_ratio = 2.0 / 3.0
viscosity_exponent = 0.19
rarefaction_ratio = 100.0
courant = 0.9
dt = courant / (1.5 * (NVX - 1) * velocity_step)
weight = velocity_step**3
centre = (NVX - 1) / 2.0

F32 = jnp.float32


def lane_velocities(rows=1):
    lane = lax.broadcasted_iota(jnp.int32, (rows, LANES), 1)
    cy = ((lane >> 4).astype(F32) - centre) * velocity_step
    cz = ((lane & (NVX - 1)).astype(F32) - centre) * velocity_step
    return cy, cz


def own_cx():
    return (lax.axis_index("vel").astype(F32) - centre) * velocity_step


def maxwellian(rho, ux, temperature, cx, cy, cz):
    width = (cx - ux) * (cx - ux) + cy * cy + cz * cz
    return rho * (2.0 * math.pi * temperature) ** (-1.5) * jnp.exp(width * (-0.5 / temperature))


def store_faces(filled, faces):
    _, cz = lane_velocities(GROUPS)
    positive = lax.axis_index("vel") >= NVX // 2
    first = pl.multiple_of(jnp.where(positive, (BS - 1) * GROUPS, 0), GROUPS)
    for half in range(2):
        faces[half, 0] = filled[half, pl.ds(first, GROUPS), :]
        for i in range(BS):
            row = i * GROUPS + half * (BS - 1) * BS
            faces[half, 1, i * BS : (i + 1) * BS, :] = filled[half, row : row + BS, :]
        bottom = filled[half, pl.ds(0, GROUPS, stride=BS), :]
        top = filled[half, pl.ds(BS - 1, GROUPS, stride=BS), :]
        upward = cz[:, half * HALF : (half + 1) * HALF] > 0
        faces[half, 2] = jnp.where(upward, top, bottom)


PIECES = 4
PIECE = CELLS // PIECES


def fill_kernel(dist_hbm, solid_hbm, filled, faces, dist, solid, sems):
    flags_copy = pltpu.make_async_copy(solid_hbm, solid, sems.at[PIECES])
    flags_copy.start()
    copies = []
    for piece in range(PIECES):
        at = pl.ds(piece * PIECE, PIECE)
        copies.append(pltpu.make_async_copy(dist_hbm.at[at], dist.at[at], sems.at[piece]))
        copies[-1].start()
    cx = own_cx()
    cy, cz = lane_velocities()
    wall = maxwellian(20.0, 0.0, 2.0, cx, cy, cz)
    top = lax.broadcasted_iota(jnp.int32, (BS, HALF), 0) == 0
    flags_copy.wait()
    flags = jnp.broadcast_to(solid[...].astype(F32), (BS, CELLS))
    mask = lax.dot_general(
        flags, top.astype(F32), (((0,), (0,)), ((), ())), preferred_element_type=F32
    )
    for piece, copy in enumerate(copies):
        copy.wait()
        at = slice(piece * PIECE, (piece + 1) * PIECE)
        for half in range(2):
            lanes = slice(half * HALF, (half + 1) * HALF)
            filled[half, at] = jnp.where(mask[at] > 0.5, wall[:, lanes], dist[at, lanes])
    store_faces(filled, faces)


def upwind_edge(cz, sub):
    upward = jnp.broadcast_to(cz > 0, (BS, HALF))
    return upward, (sub == 0) & upward | (sub == BS - 1) & jnp.logical_not(upward)


def cell_basis():
    cy, cz = lane_velocities(NVX)
    row = lax.broadcasted_iota(jnp.int32, (NVX, LANES), 0)
    zero = jnp.zeros((NVX, LANES), F32)

    def rows(first, entries):
        out = zero
        for k, entry in enumerate(entries):
            out = jnp.where(row == first + k, entry, out)
        return out

    exponent = rows(0, [cy * cy + cz * cz, cy, cz, 1.0])
    flow = rows(4, [cy, cz, 1.0])
    stay = rows(7, [1.0])[:, :HALF]
    top = rows(8, [1.0])[:, :HALF]
    block = jnp.concatenate([exponent, flow, stay, top], axis=1)
    return jnp.concatenate([block] * 3, axis=0).astype(jnp.bfloat16)


def inner_kernel(filled, inner, basis=None):
    if basis is not None:
        basis[...] = cell_basis()
    cx = own_cx()
    cy, cz = lane_velocities()
    positive = lax.axis_index("vel") >= NVX // 2
    kx = dt * jnp.abs(cx)
    ky = dt * jnp.abs(cy)
    kz = dt * jnp.abs(cz)
    keep = 1.0 - kx - ky - kz
    sub = lax.broadcasted_iota(jnp.int32, (BS, HALF), 0)
    for half in range(2):
        lanes = slice(half * HALF, (half + 1) * HALF)
        upward, edge = upwind_edge(cz[:, lanes], sub)
        k0 = jnp.broadcast_to(keep[:, lanes], (BS, HALF))
        k2 = jnp.broadcast_to(ky[:, lanes], (BS, HALF))
        k3 = jnp.where(edge, 0.0, jnp.broadcast_to(kz[:, lanes], (BS, HALF)))
        low_x = jnp.where(positive, kx, 0.0)
        high_x = jnp.where(positive, 0.0, kx)
        for i in range(BS):
            for j in range(BS):
                row = (i * BS + j) * BS
                value = filled[half, row : row + BS]
                total = k0 * value
                if i > 0:
                    total = total + low_x * filled[half, row - GROUPS : row - GROUPS + BS]
                if i < BS - 1:
                    total = total + high_x * filled[half, row + GROUPS : row + GROUPS + BS]
                if half == 0 and j < BS - 1:
                    total = total + k2 * filled[half, row + BS : row + 2 * BS]
                if half == 1 and j > 0:
                    total = total + k2 * filled[half, row - BS : row]
                z_up = jnp.where(upward, pltpu.roll(value, 1, 0), pltpu.roll(value, BS - 1, 0))
                inner[half, row : row + BS] = total + k3 * z_up


def ghost_kernel(neighbours, inner, own, below, above, advected, partial, ghost_z):
    cx = own_cx()
    cy, cz = lane_velocities()
    here = lax.axis_index("space")
    count = lax.axis_size("space")
    inflow = maxwellian(20.0, 2.5, 1.0, cx, cy, cz)

    block = neighbours[...]
    places = jnp.where(block < 0, 3, lax.rem(block - here + 1 + count, count))

    def pick(place, dim, half):
        place = jnp.broadcast_to(place, (GROUPS, HALF))
        value = jnp.where(place == 0, below[half, dim], above[half, dim])
        value = jnp.where(place == 1, own[half, dim], value)
        return jnp.where(place == 3, inflow[:, half * HALF : (half + 1) * HALF], value)

    positive = lax.axis_index("vel") >= NVX // 2
    face = [places[:, k : k + 1] for k in range(6)]
    face_x = jnp.where(positive, face[0], face[1])
    first = pl.multiple_of(jnp.where(positive, 0, (BS - 1) * GROUPS), GROUPS)
    kx = dt * jnp.abs(cx)
    ky = dt * jnp.abs(cy)
    kz = dt * jnp.abs(cz)
    sub = lax.broadcasted_iota(jnp.int32, (BS, HALF), 0)
    one = jnp.ones_like(cy)
    plane = cy * cy + cz * cz
    table = weight * jnp.concatenate(
        [one, cy, cz, cy * cy, cz * cz, cy * cz, cy * plane, cz * plane], axis=0
    )
    coarse = table.astype(jnp.bfloat16)
    table = jnp.concatenate([coarse.astype(F32), table - coarse.astype(F32)], axis=0)
    table = table.astype(jnp.bfloat16)
    total = jnp.zeros((2 * BS, CELLS), F32)
    for half in range(2):
        lanes = slice(half * HALF, (half + 1) * HALF)
        _, edge = upwind_edge(cz[:, lanes], sub)
        side = edge.astype(F32)
        up64 = jnp.broadcast_to(cz[:, lanes] > 0, (GROUPS, HALF))
        ghost_z[half] = kz[:, lanes] * jnp.where(up64, pick(face[4], 2, half), pick(face[5], 2, half))
        gy = ky[:, lanes] * pick(face[3 - half], 1, half)
        gx = kx * pick(face_x, 0, half)
        for i in range(BS):
            for j in range(BS):
                group = i * BS + j
                at = slice(group * BS, (group + 1) * BS)
                z_ghost = jnp.broadcast_to(ghost_z[half, group : group + 1], (BS, HALF))
                value = inner[half, at] + side * z_ghost
                if j == (BS - 1 if half == 0 else 0):
                    value = value + gy[i * BS : (i + 1) * BS]
                advected[half, at] = value
        rows = pl.ds(first, GROUPS)
        advected[half, rows] = advected[half, rows] + gx
        value = advected[half]
        high = value.astype(jnp.bfloat16)
        low = (value - high.astype(F32)).astype(jnp.bfloat16)
        for piece in (high, low):
            total = total + lax.dot_general(
                table[:, lanes],
                piece,
                (((1,), (1,)), ((), ())),
                preferred_element_type=F32,
            )
    partial[...] = jnp.broadcast_to(total[:BS] + total[BS:], (NVX, BS, CELLS))


def bfloat_pieces(value):
    pieces = []
    for _ in range(3):
        piece = value.astype(jnp.bfloat16).astype(F32)
        pieces.append(piece)
        value = value - piece
    return pieces


def collide(gathered, solid, advected, basis, turned, sizes, store):
    sums = [None] * 4
    for a in range(NVX // 2, NVX):
        ca = (a - centre) * velocity_step
        high, low = gathered[a], gathered[NVX - 1 - a]
        even, odd = high + low, high - low
        terms = [even, ca * odd, ca**2 * even, ca**3 * odd]
        sums = [t if s is None else s + t for s, t in zip(sums, terms)]

    def row(n, r):
        return sums[n][r : r + 1, :]

    rho = row(0, 0)
    jx, jy, jz = row(1, 0), row(0, 1), row(0, 2)
    pxx, pyy, pzz = row(2, 0), row(0, 3), row(0, 4)
    pxy, pxz, pyz = row(1, 1), row(1, 2), row(0, 5)
    hx = row(3, 0) + row(1, 3) + row(1, 4)
    hy = row(2, 1) + row(0, 6)
    hz = row(2, 2) + row(0, 7)
    energy = pxx + pyy + pzz
    inverse = 1.0 / rho
    ux, uy, uz = jx * inverse, jy * inverse, jz * inverse
    speed = ux * ux + uy * uy + uz * uz
    temperature = (energy * inverse - speed) / 3.0
    twice = 2.0 * rho * speed - energy
    qx = hx - 2.0 * (ux * pxx + uy * pxy + uz * pxz) + ux * twice
    qy = hy - 2.0 * (ux * pxy + uy * pyy + uz * pyz) + uy * twice
    qz = hz - 2.0 * (ux * pxz + uy * pyz + uz * pzz) + uz * twice
    log_t = jnp.log(temperature)
    cold = 1.0 / temperature
    rate = (dt / rarefaction_ratio) * rho * jnp.exp(viscosity_exponent * log_t)
    keep = 1.0 / (1.0 + rate)
    amount = rate * keep * rho * (2.0 * math.pi) ** (-1.5) * jnp.exp(-1.5 * log_t)
    scale = ((1.0 - diffusivity_ratio) / 5.0) * inverse * cold * cold
    cx = own_cx()
    rx = cx - ux
    slope = -0.5 * cold
    sy, sz = qy * scale, qz * scale
    inside = solid[...] == 1
    wall_amount = 20.0 * (2.0 * math.pi * 2.0) ** (-1.5)
    rows = [
        jnp.where(inside, -0.25, slope),
        jnp.where(inside, 0.0, cold * uy),
        jnp.where(inside, 0.0, cold * uz),
        jnp.where(inside, -0.25 * (cx * cx), slope * (rx * rx + uy * uy + uz * uz)),
        jnp.where(inside, 0.0, sy),
        jnp.where(inside, 0.0, sz),
        jnp.where(inside, 0.0, rx * qx * scale - sy * uy - sz * uz),
        jnp.where(inside, 0.0, keep),
        jnp.where(inside, wall_amount, amount),
    ]
    rows = rows + [jnp.zeros_like(rho)] * (NVX - len(rows))
    pieces = jnp.concatenate(bfloat_pieces(jnp.concatenate(rows, axis=0)), axis=0)
    turned[...] = pieces.T.astype(jnp.bfloat16)
    first = 0
    for chunk in sizes:
        at = slice(first, first + chunk)
        wide = jnp.dot(turned[at], basis[...], preferred_element_type=F32)
        stay = wide[:, 2 * LANES : 2 * LANES + HALF]
        top = wide[:, 2 * LANES + HALF :]
        for half in range(2):
            exponent = wide[:, half * HALF : (half + 1) * HALF]
            flow = wide[:, LANES + half * HALF : LANES + (half + 1) * HALF]
            shape = 1.0 + flow * (-2.0 * exponent - 5.0)
            value = stay * advected[half, at] + top * jnp.exp(exponent) * shape
            store(half, first, chunk, value)
        first += chunk


def collide_kernel(gathered, solid, advected, basis, filled, faces, turned):
    def store(half, first, count, value):
        filled[half, first : first + count] = value

    collide(gathered, solid, advected, basis, turned, [PIECE] * PIECES, store)
    store_faces(filled, faces)


def last_kernel(gathered, solid, advected, basis, result, turned, out, sems):
    copies = []

    def store(half, first, count, value):
        out[first : first + count, half * HALF : (half + 1) * HALF] = value
        if half == 1:
            at = pl.ds(first, count)
            copy = pltpu.make_async_copy(out.at[at], result.at[at], sems.at[len(copies)])
            copy.start()
            copies.append(copy)

    collide(gathered, solid, advected, basis, turned, LAST_SIZES, store)
    for copy in copies:
        copy.wait()


VMEM = pl.BlockSpec(memory_space=pltpu.VMEM)
HBM = pl.BlockSpec(memory_space=pltpu.HBM)
FIELD = jax.ShapeDtypeStruct((2, CELLS, HALF), F32)
RESULT = jax.ShapeDtypeStruct((CELLS, LANES), F32)
FACES = jax.ShapeDtypeStruct((2, 3, GROUPS, HALF), F32)
PARTIAL = jax.ShapeDtypeStruct((NVX, BS, CELLS), F32)
LAST_SIZES = (176, 160, 112, 64)
BASIS = jax.ShapeDtypeStruct((3 * NVX, 3 * LANES), jnp.bfloat16)
TURNED = pltpu.VMEM((CELLS, 3 * NVX), jnp.bfloat16)


def call(kernel, ins, outs, scratch=(), out_spec=VMEM):
    size = CELLS * LANES
    return pl.pallas_call(
        kernel,
        in_specs=ins,
        out_specs=[out_spec] * len(outs),
        out_shape=outs,
        scratch_shapes=list(scratch),
        cost_estimate=pl.CostEstimate(
            flops=40 * size, transcendentals=size, bytes_accessed=8 * size
        ),
        compiler_params=pltpu.CompilerParams(vmem_limit_bytes=16 * 1024 * 1024),
    )


def on_device(dist, neighbours, solid):
    count = lax.axis_size("space")
    forward = [(i, (i + 1) % count) for i in range(count)]
    backward = [(target, source) for source, target in forward]
    filled, faces = call(
        fill_kernel,
        [HBM] * 2,
        [FIELD, FACES],
        [
            pltpu.VMEM((CELLS, LANES), F32),
            pltpu.VMEM((1, CELLS), jnp.int32),
            pltpu.SemaphoreType.DMA((PIECES + 1,)),
        ],
    )(
        pltpu.with_memory_space_constraint(dist[0], pltpu.HBM),
        pltpu.with_memory_space_constraint(solid, pltpu.HBM),
    )
    for step in range(ITERS):
        below = lax.ppermute(faces, "space", forward)
        above = lax.ppermute(faces, "space", backward)
        if step == 0:
            inner, basis = call(inner_kernel, [VMEM], [FIELD, BASIS])(filled)
        else:
            (inner,) = call(inner_kernel, [VMEM], [FIELD])(filled)
        advected, partial = call(
            ghost_kernel,
            [VMEM] * 5,
            [FIELD, PARTIAL],
            [pltpu.VMEM((2, GROUPS, HALF), F32)],
        )(neighbours, inner, faces, below, above)
        gathered = lax.all_to_all(partial, "vel", 0, 0, tiled=True)
        if step < ITERS - 1:
            filled, faces = call(collide_kernel, [VMEM] * 4, [FIELD, FACES], [TURNED])(
                gathered, solid, advected, basis
            )
        else:
            (filled,) = call(
                last_kernel,
                [VMEM] * 4,
                [RESULT],
                [TURNED, pltpu.VMEM((CELLS, LANES), F32), pltpu.SemaphoreType.DMA((4,))],
                HBM,
            )(gathered, solid, advected, basis)
    return filled[None]


def solution(mesh):
    in_specs = (P("space", None, "vel"), P("space", None), P("space", None))
    out_specs = P("space", None, "vel")
    return jax.shard_map(
        on_device, mesh=mesh, in_specs=in_specs, out_specs=out_specs, check_vma=False
    )
```

```python
import math

import jax
import jax.numpy as jnp
from jax import lax
from jax.experimental import pallas as pl
from jax.experimental.pallas import tpu as pltpu
from jax.sharding import PartitionSpec as P


NVX = 16
BS = 8
ITERS = 2
CELLS = BS * BS * BS
GROUPS = BS * BS
LANES = NVX * NVX
HALF = LANES // 2

velocity_step = 0.5
diffusivity_ratio = 2.0 / 3.0
viscosity_exponent = 0.19
rarefaction_ratio = 100.0
courant = 0.9
dt = courant / (1.5 * (NVX - 1) * velocity_step)
weight = velocity_step**3
centre = (NVX - 1) / 2.0

F32 = jnp.float32


def lane_velocities(rows=1):
    lane = lax.broadcasted_iota(jnp.int32, (rows, LANES), 1)
    cy = ((lane >> 4).astype(F32) - centre) * velocity_step
    cz = ((lane & (NVX - 1)).astype(F32) - centre) * velocity_step
    return cy, cz


def own_cx():
    return (lax.axis_index("vel").astype(F32) - centre) * velocity_step


def maxwellian(rho, ux, temperature, cx, cy, cz):
    width = (cx - ux) * (cx - ux) + cy * cy + cz * cz
    return rho * (2.0 * math.pi * temperature) ** (-1.5) * jnp.exp(width * (-0.5 / temperature))


def store_faces(filled, faces):
    _, cz = lane_velocities(GROUPS)
    positive = lax.axis_index("vel") >= NVX // 2
    first = pl.multiple_of(jnp.where(positive, (BS - 1) * GROUPS, 0), GROUPS)
    for half in range(2):
        faces[half, 0] = filled[half, pl.ds(first, GROUPS), :]
        for i in range(BS):
            row = i * GROUPS + half * (BS - 1) * BS
            faces[half, 1, i * BS : (i + 1) * BS, :] = filled[half, row : row + BS, :]
        bottom = filled[half, pl.ds(0, GROUPS, stride=BS), :]
        top = filled[half, pl.ds(BS - 1, GROUPS, stride=BS), :]
        upward = cz[:, half * HALF : (half + 1) * HALF] > 0
        faces[half, 2] = jnp.where(upward, top, bottom)


PIECES = 4
PIECE = CELLS // PIECES


def two_pieces(value):
    high = value.astype(jnp.bfloat16)
    return high, (value - high.astype(F32)).astype(jnp.bfloat16)


def moment_table():
    cy, cz = lane_velocities()
    plane = cy * cy + cz * cz
    table = weight * jnp.concatenate(
        [jnp.ones_like(cy), cy, cz, cy * cy, cz * cz, cy * cz, cy * plane, cz * plane], axis=0
    )
    return jnp.concatenate([piece.astype(F32) for piece in two_pieces(table)], axis=0)


def times_transposed(table, value):
    total = None
    for piece in two_pieces(value):
        term = lax.dot_general(
            table, piece, (((1,), (1,)), ((), ())), preferred_element_type=F32
        )
        total = term if total is None else total + term
    return total


def flux_moments(layer, flux):
    kx = dt * jnp.abs(own_cx())
    cy, cz = lane_velocities()
    ky, kz = dt * jnp.abs(cy), dt * jnp.abs(cz)
    table = moment_table()
    rising = jnp.broadcast_to(cz > 0, table.shape)
    ups, downs = [], []
    for half in range(2):
        lanes = slice(half * HALF, (half + 1) * HALF)
        rows = jnp.concatenate(
            [layer(half, 0) * kx, layer(half, 1) * ky[:, lanes], layer(half, 2) * kz[:, lanes]],
            axis=0,
        )
        both = jnp.concatenate(
            [
                jnp.where(rising[:, lanes], table[:, lanes], 0.0),
                jnp.where(rising[:, lanes], 0.0, table[:, lanes]),
            ],
            axis=0,
        )
        term = times_transposed(both.astype(jnp.bfloat16), rows)
        ups.append(term[0:BS] + term[BS : 2 * BS])
        downs.append(term[2 * BS : 3 * BS] + term[3 * BS :])
    sums = [up + down for up, down in zip(ups, downs)]
    along_x = (sums[0] + sums[1])[:, :GROUPS]
    flux[0, :, :GROUPS] = along_x
    flux[0, :, GROUPS:] = jnp.zeros_like(along_x)
    flux[1, :, :GROUPS] = sums[0][:, GROUPS : 2 * GROUPS]
    flux[1, :, GROUPS:] = sums[1][:, GROUPS : 2 * GROUPS]
    flux[2, :, :GROUPS] = (ups[0] + ups[1])[:, 2 * GROUPS :]
    flux[2, :, GROUPS:] = (downs[0] + downs[1])[:, 2 * GROUPS :]


def face_flux(faces, flux):
    flux_moments(lambda half, dim: faces[half, dim], flux)


def fill_kernel(dist_hbm, solid_hbm, filled, faces, flux, solid, dist, sems):
    copies = [
        pltpu.make_async_copy(solid_hbm, solid, sems.at[0]),
        pltpu.make_async_copy(dist_hbm, dist, sems.at[1]),
    ]
    for copy in copies:
        copy.start()
    cx = own_cx()
    cy, cz = lane_velocities()
    wall = maxwellian(20.0, 0.0, 2.0, cx, cy, cz)
    top = lax.broadcasted_iota(jnp.int32, (BS, HALF), 0) == 0
    copies[0].wait()
    flags = jnp.broadcast_to(solid[...].astype(F32), (BS, CELLS))
    mask = lax.dot_general(
        flags, top.astype(F32), (((0,), (0,)), ((), ())), preferred_element_type=F32
    )
    inside = mask > 0.5
    copies[1].wait()
    for half in range(2):
        lanes = slice(half * HALF, (half + 1) * HALF)
        filled[half] = jnp.where(inside, wall[:, lanes], dist[:, lanes])
    store_faces(filled, faces)
    face_flux(faces, flux)


def upwind_edge(cz, sub):
    upward = jnp.broadcast_to(cz > 0, (BS, HALF))
    return upward, (sub == 0) & upward | (sub == BS - 1) & jnp.logical_not(upward)


def spread_table():
    row = lax.broadcasted_iota(jnp.int32, (2 * GROUPS, CELLS), 0)
    cell = lax.broadcasted_iota(jnp.int32, (2 * GROUPS, CELLS), 1)
    place = row & (GROUPS - 1)
    later = row >= GROUPS
    positive = lax.axis_index("vel") >= NVX // 2
    first = jnp.where(positive, 0, (BS - 1) * GROUPS)
    along_x = jnp.where(later, -1, first + place)
    along_y = (place >> 3) * GROUPS + (place & (BS - 1)) + jnp.where(later, 0, GROUPS - BS)
    along_z = place * BS + jnp.where(later, BS - 1, 0)
    hits = [(cell == target).astype(F32) for target in (along_x, along_y, along_z)]
    return jnp.concatenate(hits, axis=0).astype(jnp.bfloat16)


def cell_basis():
    cy, cz = lane_velocities(NVX)
    row = lax.broadcasted_iota(jnp.int32, (NVX, LANES), 0)
    zero = jnp.zeros((NVX, LANES), F32)

    def rows(first, entries):
        out = zero
        for k, entry in enumerate(entries):
            out = jnp.where(row == first + k, entry, out)
        return out

    exponent = rows(0, [cy * cy + cz * cz, cy, cz, 1.0])
    flow = rows(4, [cy, cz, 1.0])
    stay = rows(7, [1.0])[:, :HALF]
    top = rows(8, [1.0])[:, :HALF]
    block = jnp.concatenate([exponent, flow, stay, top], axis=1)
    return jnp.concatenate([block] * 3, axis=0).astype(jnp.bfloat16)


def first_inner_kernel(filled, inner, local, basis, spread, open_flux):
    basis[...] = cell_basis()
    spread[...] = spread_table()
    cy, cz = lane_velocities()
    inflow = maxwellian(20.0, 2.5, 1.0, own_cx(), cy, cz)
    wide = jnp.broadcast_to(inflow, (GROUPS, LANES))
    flux_moments(lambda half, dim: wide[:, half * HALF : (half + 1) * HALF], open_flux)
    inner_kernel(filled, inner, local)


def inner_kernel(filled, inner, local):
    cx = own_cx()
    cy, cz = lane_velocities()
    positive = lax.axis_index("vel") >= NVX // 2
    kx = dt * jnp.abs(cx)
    ky = dt * jnp.abs(cy)
    kz = dt * jnp.abs(cz)
    keep = 1.0 - kx - ky - kz
    sub = lax.broadcasted_iota(jnp.int32, (BS, HALF), 0)
    for half in range(2):
        lanes = slice(half * HALF, (half + 1) * HALF)
        upward, edge = upwind_edge(cz[:, lanes], sub)
        k0 = jnp.broadcast_to(keep[:, lanes], (BS, HALF))
        k2 = jnp.broadcast_to(ky[:, lanes], (BS, HALF))
        k3 = jnp.where(edge, 0.0, jnp.broadcast_to(kz[:, lanes], (BS, HALF)))
        low_x = jnp.where(positive, kx, 0.0)
        high_x = jnp.where(positive, 0.0, kx)
        for i in range(BS):
            for j in range(BS):
                row = (i * BS + j) * BS
                value = filled[half, row : row + BS]
                total = k0 * value
                if i > 0:
                    total = total + low_x * filled[half, row - GROUPS : row - GROUPS + BS]
                if i < BS - 1:
                    total = total + high_x * filled[half, row + GROUPS : row + GROUPS + BS]
                if half == 0 and j < BS - 1:
                    total = total + k2 * filled[half, row + BS : row + 2 * BS]
                if half == 1 and j > 0:
                    total = total + k2 * filled[half, row - BS : row]
                z_up = jnp.where(upward, pltpu.roll(value, 1, 0), pltpu.roll(value, BS - 1, 0))
                inner[half, row : row + BS] = total + k3 * z_up
    table = moment_table().astype(jnp.bfloat16)
    total = times_transposed(table[:, :HALF], inner[0])
    total = total + times_transposed(table[:, HALF:], inner[1])
    local[...] = total[:BS] + total[BS:]


def source_places(neighbours):
    block = neighbours[...]
    here = lax.axis_index("space")
    count = lax.axis_size("space")
    places = jnp.where(block < 0, 3, lax.rem(block - here + 1 + count, count))
    face = [places[:, k : k + 1] for k in range(6)]
    positive = lax.axis_index("vel") >= NVX // 2
    return face, jnp.where(positive, face[0], face[1])


def choose(place, below, own, above, opened):
    value = jnp.where(place == 0, below, above)
    value = jnp.where(place == 1, own, value)
    return jnp.where(place == 3, opened, value)


def join_kernel(neighbours, local, own, below, above, opened, spread, partial):
    face, face_x = source_places(neighbours)
    early = lax.broadcasted_iota(jnp.int32, (BS, 2 * GROUPS), 1) < GROUPS
    places = [
        jnp.broadcast_to(face_x, early.shape),
        jnp.where(early, face[3], face[2]),
        jnp.where(early, face[4], face[5]),
    ]
    columns = []
    for dim, place in enumerate(places):
        value = choose(place, below[dim], own[dim], above[dim], opened[dim])
        pieces = bfloat_pieces(value)
        columns.append(jnp.concatenate(pieces + [jnp.zeros_like(value)], axis=0))
    left = jnp.concatenate(columns, axis=1).astype(jnp.bfloat16)
    added = jnp.dot(left, spread[...], preferred_element_type=F32)
    total = local[...] + (added[:BS] + added[BS : 2 * BS] + added[2 * BS : 3 * BS])
    partial[...] = jnp.broadcast_to(total, (NVX, BS, CELLS))


def ghost_kernel(neighbours, inner, own, below, above, advected, ghost_z):
    cx = own_cx()
    cy, cz = lane_velocities()
    inflow = maxwellian(20.0, 2.5, 1.0, cx, cy, cz)
    face, face_x = source_places(neighbours)

    def pick(place, dim, half):
        place = jnp.broadcast_to(place, (GROUPS, HALF))
        opened = inflow[:, half * HALF : (half + 1) * HALF]
        return choose(place, below[half, dim], own[half, dim], above[half, dim], opened)

    positive = lax.axis_index("vel") >= NVX // 2
    first = pl.multiple_of(jnp.where(positive, 0, (BS - 1) * GROUPS), GROUPS)
    kx = dt * jnp.abs(cx)
    ky = dt * jnp.abs(cy)
    kz = dt * jnp.abs(cz)
    sub = lax.broadcasted_iota(jnp.int32, (BS, HALF), 0)
    for half in range(2):
        lanes = slice(half * HALF, (half + 1) * HALF)
        _, edge = upwind_edge(cz[:, lanes], sub)
        side = edge.astype(F32)
        up64 = jnp.broadcast_to(cz[:, lanes] > 0, (GROUPS, HALF))
        ghost_z[half] = kz[:, lanes] * jnp.where(up64, pick(face[4], 2, half), pick(face[5], 2, half))
        gy = ky[:, lanes] * pick(face[3 - half], 1, half)
        gx = kx * pick(face_x, 0, half)
        for i in range(BS):
            for j in range(BS):
                group = i * BS + j
                at = slice(group * BS, (group + 1) * BS)
                z_ghost = jnp.broadcast_to(ghost_z[half, group : group + 1], (BS, HALF))
                value = inner[half, at] + side * z_ghost
                if j == (BS - 1 if half == 0 else 0):
                    value = value + gy[i * BS : (i + 1) * BS]
                advected[half, at] = value
        rows = pl.ds(first, GROUPS)
        advected[half, rows] = advected[half, rows] + gx


def bfloat_pieces(value):
    pieces = []
    for _ in range(3):
        piece = value.astype(jnp.bfloat16).astype(F32)
        pieces.append(piece)
        value = value - piece
    return pieces


def collide(gathered, solid, advected, basis, turned, sizes, store):
    sums = [None] * 4
    for a in range(NVX // 2, NVX):
        ca = (a - centre) * velocity_step
        high, low = gathered[a], gathered[NVX - 1 - a]
        even, odd = high + low, high - low
        terms = [even, ca * odd, ca**2 * even, ca**3 * odd]
        sums = [t if s is None else s + t for s, t in zip(sums, terms)]

    def row(n, r):
        return sums[n][r : r + 1, :]

    rho = row(0, 0)
    jx, jy, jz = row(1, 0), row(0, 1), row(0, 2)
    pxx, pyy, pzz = row(2, 0), row(0, 3), row(0, 4)
    pxy, pxz, pyz = row(1, 1), row(1, 2), row(0, 5)
    hx = row(3, 0) + row(1, 3) + row(1, 4)
    hy = row(2, 1) + row(0, 6)
    hz = row(2, 2) + row(0, 7)
    energy = pxx + pyy + pzz
    inverse = 1.0 / rho
    ux, uy, uz = jx * inverse, jy * inverse, jz * inverse
    speed = ux * ux + uy * uy + uz * uz
    temperature = (energy * inverse - speed) / 3.0
    twice = 2.0 * rho * speed - energy
    qx = hx - 2.0 * (ux * pxx + uy * pxy + uz * pxz) + ux * twice
    qy = hy - 2.0 * (ux * pxy + uy * pyy + uz * pyz) + uy * twice
    qz = hz - 2.0 * (ux * pxz + uy * pyz + uz * pzz) + uz * twice
    log_t = jnp.log(temperature)
    cold = 1.0 / temperature
    rate = (dt / rarefaction_ratio) * rho * jnp.exp(viscosity_exponent * log_t)
    keep = 1.0 / (1.0 + rate)
    amount = rate * keep * rho * (2.0 * math.pi) ** (-1.5) * jnp.exp(-1.5 * log_t)
    scale = ((1.0 - diffusivity_ratio) / 5.0) * inverse * cold * cold
    cx = own_cx()
    rx = cx - ux
    slope = -0.5 * cold
    sy, sz = qy * scale, qz * scale
    inside = solid[...] == 1
    wall_amount = 20.0 * (2.0 * math.pi * 2.0) ** (-1.5)
    rows = [
        jnp.where(inside, -0.25, slope),
        jnp.where(inside, 0.0, cold * uy),
        jnp.where(inside, 0.0, cold * uz),
        jnp.where(inside, -0.25 * (cx * cx), slope * (rx * rx + uy * uy + uz * uz)),
        jnp.where(inside, 0.0, sy),
        jnp.where(inside, 0.0, sz),
        jnp.where(inside, 0.0, rx * qx * scale - sy * uy - sz * uz),
        jnp.where(inside, 0.0, keep),
        jnp.where(inside, wall_amount, amount),
    ]
    rows = rows + [jnp.zeros_like(rho)] * (NVX - len(rows))
    pieces = jnp.concatenate(bfloat_pieces(jnp.concatenate(rows, axis=0)), axis=0)
    turned[...] = pieces.T.astype(jnp.bfloat16)
    first = 0
    for chunk in sizes:
        at = slice(first, first + chunk)
        wide = jnp.dot(turned[at], basis[...], preferred_element_type=F32)
        stay = wide[:, 2 * LANES : 2 * LANES + HALF]
        top = wide[:, 2 * LANES + HALF :]
        for half in range(2):
            exponent = wide[:, half * HALF : (half + 1) * HALF]
            flow = wide[:, LANES + half * HALF : LANES + (half + 1) * HALF]
            shape = 1.0 + flow * (-2.0 * exponent - 5.0)
            value = stay * advected[half, at] + top * jnp.exp(exponent) * shape
            store(half, first, chunk, value)
        first += chunk


def collide_kernel(gathered, solid, advected, basis, filled, faces, flux, turned):
    def store(half, first, count, value):
        filled[half, first : first + count] = value

    collide(gathered, solid, advected, basis, turned, [PIECE] * PIECES, store)
    store_faces(filled, faces)
    face_flux(faces, flux)


def last_kernel(gathered, solid, advected, basis, result, turned, out, sems):
    copies = []

    def store(half, first, count, value):
        out[first : first + count, half * HALF : (half + 1) * HALF] = value
        if half == 1:
            at = pl.ds(first, count)
            copy = pltpu.make_async_copy(out.at[at], result.at[at], sems.at[len(copies)])
            copy.start()
            copies.append(copy)

    collide(gathered, solid, advected, basis, turned, LAST_SIZES, store)
    for copy in copies:
        copy.wait()


VMEM = pl.BlockSpec(memory_space=pltpu.VMEM)
HBM = pl.BlockSpec(memory_space=pltpu.HBM)
FIELD = jax.ShapeDtypeStruct((2, CELLS, HALF), F32)
RESULT = jax.ShapeDtypeStruct((CELLS, LANES), F32)
FACES = jax.ShapeDtypeStruct((2, 3, GROUPS, HALF), F32)
SPREAD = jax.ShapeDtypeStruct((6 * GROUPS, CELLS), jnp.bfloat16)
FLUX = jax.ShapeDtypeStruct((3, BS, 2 * GROUPS), F32)
LOCAL = jax.ShapeDtypeStruct((BS, CELLS), F32)
SOLID = jax.ShapeDtypeStruct((1, CELLS), jnp.int32)
PARTIAL = jax.ShapeDtypeStruct((NVX, BS, CELLS), F32)
LAST_SIZES = (176, 160, 112, 64)
BASIS = jax.ShapeDtypeStruct((3 * NVX, 3 * LANES), jnp.bfloat16)
TURNED = pltpu.VMEM((CELLS, 3 * NVX), jnp.bfloat16)


def call(kernel, ins, outs, scratch=(), out_spec=VMEM):
    size = CELLS * LANES
    return pl.pallas_call(
        kernel,
        in_specs=ins,
        out_specs=[out_spec] * len(outs),
        out_shape=outs,
        scratch_shapes=list(scratch),
        cost_estimate=pl.CostEstimate(
            flops=40 * size, transcendentals=size, bytes_accessed=8 * size
        ),
        compiler_params=pltpu.CompilerParams(vmem_limit_bytes=16 * 1024 * 1024),
    )


def on_device(dist, neighbours, solid):
    count = lax.axis_size("space")
    forward = [(i, (i + 1) % count) for i in range(count)]
    backward = [(target, source) for source, target in forward]
    filled, faces, flux, solid = call(
        fill_kernel,
        [HBM] * 2,
        [FIELD, FACES, FLUX, SOLID],
        [pltpu.VMEM((CELLS, LANES), F32), pltpu.SemaphoreType.DMA((2,))],
    )(
        pltpu.with_memory_space_constraint(dist[0], pltpu.HBM),
        pltpu.with_memory_space_constraint(solid, pltpu.HBM),
    )
    for step in range(ITERS):
        flux_below = lax.ppermute(flux, "space", forward)
        below = lax.ppermute(faces, "space", forward)
        flux_above = lax.ppermute(flux, "space", backward)
        above = lax.ppermute(faces, "space", backward)
        if step == 0:
            inner, local, basis, spread, open_flux = call(
                first_inner_kernel, [VMEM], [FIELD, LOCAL, BASIS, SPREAD, FLUX]
            )(filled)
        else:
            inner, local = call(inner_kernel, [VMEM], [FIELD, LOCAL])(filled)
        (partial,) = call(join_kernel, [VMEM] * 7, [PARTIAL])(
            neighbours, local, flux, flux_below, flux_above, open_flux, spread
        )
        gathered = lax.all_to_all(partial, "vel", 0, 0, tiled=True)
        (advected,) = call(
            ghost_kernel, [VMEM] * 5, [FIELD], [pltpu.VMEM((2, GROUPS, HALF), F32)]
        )(neighbours, inner, faces, below, above)
        if step < ITERS - 1:
            filled, faces, flux = call(
                collide_kernel, [VMEM] * 4, [FIELD, FACES, FLUX], [TURNED]
            )(gathered, solid, advected, basis)
        else:
            (filled,) = call(
                last_kernel,
                [VMEM] * 4,
                [RESULT],
                [TURNED, pltpu.VMEM((CELLS, LANES), F32), pltpu.SemaphoreType.DMA((4,))],
                HBM,
            )(gathered, solid, advected, basis)
    return filled[None]


def solution(mesh):
    in_specs = (P("space", None, "vel"), P("space", None), P("space", None))
    out_specs = P("space", None, "vel")
    return jax.shard_map(
        on_device, mesh=mesh, in_specs=in_specs, out_specs=out_specs, check_vma=False
    )
```

```python
import math

import jax
import jax.numpy as jnp
from jax import lax
from jax.experimental import pallas as pl
from jax.experimental.pallas import tpu as pltpu
from jax.sharding import PartitionSpec as P


NVX = 16
BS = 8
ITERS = 2
CELLS = BS * BS * BS
GROUPS = BS * BS
LANES = NVX * NVX
HALF = LANES // 2

velocity_step = 0.5
diffusivity_ratio = 2.0 / 3.0
viscosity_exponent = 0.19
rarefaction_ratio = 100.0
courant = 0.9
dt = courant / (1.5 * (NVX - 1) * velocity_step)
weight = velocity_step**3
centre = (NVX - 1) / 2.0

F32 = jnp.float32


def lane_velocities(rows=1):
    lane = lax.broadcasted_iota(jnp.int32, (rows, LANES), 1)
    cy = ((lane >> 4).astype(F32) - centre) * velocity_step
    cz = ((lane & (NVX - 1)).astype(F32) - centre) * velocity_step
    return cy, cz


def own_cx():
    return (lax.axis_index("vel").astype(F32) - centre) * velocity_step


def maxwellian(rho, ux, temperature, cx, cy, cz):
    width = (cx - ux) * (cx - ux) + cy * cy + cz * cz
    return rho * (2.0 * math.pi * temperature) ** (-1.5) * jnp.exp(width * (-0.5 / temperature))


def store_faces(filled, faces):
    _, cz = lane_velocities(GROUPS)
    positive = lax.axis_index("vel") >= NVX // 2
    first = pl.multiple_of(jnp.where(positive, (BS - 1) * GROUPS, 0), GROUPS)
    for half in range(2):
        faces[half, 0] = filled[half, pl.ds(first, GROUPS), :]
        for i in range(BS):
            row = i * GROUPS + half * (BS - 1) * BS
            faces[half, 1, i * BS : (i + 1) * BS, :] = filled[half, row : row + BS, :]
        bottom = filled[half, pl.ds(0, GROUPS, stride=BS), :]
        top = filled[half, pl.ds(BS - 1, GROUPS, stride=BS), :]
        upward = cz[:, half * HALF : (half + 1) * HALF] > 0
        faces[half, 2] = jnp.where(upward, top, bottom)


PIECES = 4
PIECE = CELLS // PIECES


def two_pieces(value):
    high = value.astype(jnp.bfloat16)
    return high, (value - high.astype(F32)).astype(jnp.bfloat16)


def moment_table():
    cy, cz = lane_velocities()
    plane = cy * cy + cz * cz
    table = weight * jnp.concatenate(
        [jnp.ones_like(cy), cy, cz, cy * cy, cz * cz, cy * cz, cy * plane, cz * plane], axis=0
    )
    return jnp.concatenate([piece.astype(F32) for piece in two_pieces(table)], axis=0)


def times_transposed(table, value):
    total = None
    for piece in two_pieces(value):
        term = lax.dot_general(
            table, piece, (((1,), (1,)), ((), ())), preferred_element_type=F32
        )
        total = term if total is None else total + term
    return total


def flux_moments(layer, flux):
    kx = dt * jnp.abs(own_cx())
    cy, cz = lane_velocities()
    ky, kz = dt * jnp.abs(cy), dt * jnp.abs(cz)
    table = moment_table()
    rising = jnp.broadcast_to(cz > 0, table.shape)
    ups, downs = [], []
    for half in range(2):
        lanes = slice(half * HALF, (half + 1) * HALF)
        rows = jnp.concatenate(
            [layer(half, 0) * kx, layer(half, 1) * ky[:, lanes], layer(half, 2) * kz[:, lanes]],
            axis=0,
        )
        both = jnp.concatenate(
            [
                jnp.where(rising[:, lanes], table[:, lanes], 0.0),
                jnp.where(rising[:, lanes], 0.0, table[:, lanes]),
            ],
            axis=0,
        )
        term = times_transposed(both.astype(jnp.bfloat16), rows)
        ups.append(term[0:BS] + term[BS : 2 * BS])
        downs.append(term[2 * BS : 3 * BS] + term[3 * BS :])
    sums = [up + down for up, down in zip(ups, downs)]
    along_x = (sums[0] + sums[1])[:, :GROUPS]
    flux[0, :, :GROUPS] = along_x
    flux[0, :, GROUPS:] = jnp.zeros_like(along_x)
    flux[1, :, :GROUPS] = sums[0][:, GROUPS : 2 * GROUPS]
    flux[1, :, GROUPS:] = sums[1][:, GROUPS : 2 * GROUPS]
    flux[2, :, :GROUPS] = (ups[0] + ups[1])[:, 2 * GROUPS :]
    flux[2, :, GROUPS:] = (downs[0] + downs[1])[:, 2 * GROUPS :]


def face_flux(faces, flux):
    flux_moments(lambda half, dim: faces[half, dim], flux)


def fill_kernel(
    dist_hbm, solid_hbm, table_hbm, filled, faces, flux, solid, neighbours, dist, sems
):
    copies = [
        pltpu.make_async_copy(solid_hbm, solid, sems.at[0]),
        pltpu.make_async_copy(dist_hbm, dist, sems.at[1]),
        pltpu.make_async_copy(table_hbm, neighbours, sems.at[2]),
    ]
    for copy in copies:
        copy.start()
    cx = own_cx()
    cy, cz = lane_velocities()
    wall = maxwellian(20.0, 0.0, 2.0, cx, cy, cz)
    top = lax.broadcasted_iota(jnp.int32, (BS, HALF), 0) == 0
    copies[0].wait()
    flags = jnp.broadcast_to(solid[...].astype(F32), (BS, CELLS))
    mask = lax.dot_general(
        flags, top.astype(F32), (((0,), (0,)), ((), ())), preferred_element_type=F32
    )
    inside = mask > 0.5
    copies[1].wait()
    for half in range(2):
        lanes = slice(half * HALF, (half + 1) * HALF)
        filled[half] = jnp.where(inside, wall[:, lanes], dist[:, lanes])
    store_faces(filled, faces)
    face_flux(faces, flux)
    copies[2].wait()


def upwind_edge(cz, sub):
    upward = jnp.broadcast_to(cz > 0, (BS, HALF))
    return upward, (sub == 0) & upward | (sub == BS - 1) & jnp.logical_not(upward)


def spread_table():
    row = lax.broadcasted_iota(jnp.int32, (2 * GROUPS, CELLS), 0)
    cell = lax.broadcasted_iota(jnp.int32, (2 * GROUPS, CELLS), 1)
    place = row & (GROUPS - 1)
    later = row >= GROUPS
    positive = lax.axis_index("vel") >= NVX // 2
    first = jnp.where(positive, 0, (BS - 1) * GROUPS)
    along_x = jnp.where(later, -1, first + place)
    along_y = (place >> 3) * GROUPS + (place & (BS - 1)) + jnp.where(later, 0, GROUPS - BS)
    along_z = place * BS + jnp.where(later, BS - 1, 0)
    hits = [(cell == target).astype(F32) for target in (along_x, along_y, along_z)]
    return jnp.concatenate(hits, axis=0).astype(jnp.bfloat16)


def cell_basis():
    cy, cz = lane_velocities(NVX)
    row = lax.broadcasted_iota(jnp.int32, (NVX, LANES), 0)
    zero = jnp.zeros((NVX, LANES), F32)

    def rows(first, entries):
        out = zero
        for k, entry in enumerate(entries):
            out = jnp.where(row == first + k, entry, out)
        return out

    exponent = rows(0, [cy * cy + cz * cz, cy, cz, 1.0])
    flow = rows(4, [cy, cz, 1.0])
    stay = rows(7, [1.0])[:, :HALF]
    top = rows(8, [1.0])[:, :HALF]
    block = jnp.concatenate([exponent, flow, stay, top], axis=1)
    return jnp.concatenate([block] * 3, axis=0).astype(jnp.bfloat16)


def first_inner_kernel(filled, inner, local, basis, spread, open_flux):
    basis[...] = cell_basis()
    spread[...] = spread_table()
    cy, cz = lane_velocities()
    inflow = maxwellian(20.0, 2.5, 1.0, own_cx(), cy, cz)
    wide = jnp.broadcast_to(inflow, (GROUPS, LANES))
    flux_moments(lambda half, dim: wide[:, half * HALF : (half + 1) * HALF], open_flux)
    inner_kernel(filled, inner, local)


def inner_kernel(filled, inner, local):
    cx = own_cx()
    cy, cz = lane_velocities()
    positive = lax.axis_index("vel") >= NVX // 2
    kx = dt * jnp.abs(cx)
    ky = dt * jnp.abs(cy)
    kz = dt * jnp.abs(cz)
    keep = 1.0 - kx - ky - kz
    sub = lax.broadcasted_iota(jnp.int32, (BS, HALF), 0)
    for half in range(2):
        lanes = slice(half * HALF, (half + 1) * HALF)
        upward, edge = upwind_edge(cz[:, lanes], sub)
        k0 = jnp.broadcast_to(keep[:, lanes], (BS, HALF))
        k2 = jnp.broadcast_to(ky[:, lanes], (BS, HALF))
        k3 = jnp.where(edge, 0.0, jnp.broadcast_to(kz[:, lanes], (BS, HALF)))
        low_x = jnp.where(positive, kx, 0.0)
        high_x = jnp.where(positive, 0.0, kx)
        for i in range(BS):
            for j in range(BS):
                row = (i * BS + j) * BS
                value = filled[half, row : row + BS]
                total = k0 * value
                if i > 0:
                    total = total + low_x * filled[half, row - GROUPS : row - GROUPS + BS]
                if i < BS - 1:
                    total = total + high_x * filled[half, row + GROUPS : row + GROUPS + BS]
                if half == 0 and j < BS - 1:
                    total = total + k2 * filled[half, row + BS : row + 2 * BS]
                if half == 1 and j > 0:
                    total = total + k2 * filled[half, row - BS : row]
                z_up = jnp.where(upward, pltpu.roll(value, 1, 0), pltpu.roll(value, BS - 1, 0))
                inner[half, row : row + BS] = total + k3 * z_up
    table = moment_table().astype(jnp.bfloat16)
    total = times_transposed(table[:, :HALF], inner[0])
    total = total + times_transposed(table[:, HALF:], inner[1])
    local[...] = total[:BS] + total[BS:]


def source_places(neighbours):
    block = neighbours[...]
    here = lax.axis_index("space")
    count = lax.axis_size("space")
    places = jnp.where(block < 0, 3, lax.rem(block - here + 1 + count, count))
    face = [places[:, k : k + 1] for k in range(6)]
    positive = lax.axis_index("vel") >= NVX // 2
    return face, jnp.where(positive, face[0], face[1])


def choose(place, below, own, above, opened):
    value = jnp.where(place == 0, below, above)
    value = jnp.where(place == 1, own, value)
    return jnp.where(place == 3, opened, value)


def join_kernel(neighbours, local, own, below, above, opened, spread, partial):
    face, face_x = source_places(neighbours)
    early = lax.broadcasted_iota(jnp.int32, (BS, 2 * GROUPS), 1) < GROUPS
    places = [
        jnp.broadcast_to(face_x, early.shape),
        jnp.where(early, face[3], face[2]),
        jnp.where(early, face[4], face[5]),
    ]
    columns = []
    for dim, place in enumerate(places):
        value = choose(place, below[dim], own[dim], above[dim], opened[dim])
        pieces = bfloat_pieces(value)
        columns.append(jnp.concatenate(pieces + [jnp.zeros_like(value)], axis=0))
    left = jnp.concatenate(columns, axis=1).astype(jnp.bfloat16)
    added = jnp.dot(left, spread[...], preferred_element_type=F32)
    total = local[...] + (added[:BS] + added[BS : 2 * BS] + added[2 * BS : 3 * BS])
    partial[...] = jnp.broadcast_to(total, (NVX, BS, CELLS))


def add_ghosts(neighbours, inner, own, below, above, advected, ghost_z):
    cx = own_cx()
    cy, cz = lane_velocities()
    inflow = maxwellian(20.0, 2.5, 1.0, cx, cy, cz)
    face, face_x = source_places(neighbours)

    def pick(place, dim, half):
        place = jnp.broadcast_to(place, (GROUPS, HALF))
        opened = inflow[:, half * HALF : (half + 1) * HALF]
        return choose(place, below[half, dim], own[half, dim], above[half, dim], opened)

    positive = lax.axis_index("vel") >= NVX // 2
    first = pl.multiple_of(jnp.where(positive, 0, (BS - 1) * GROUPS), GROUPS)
    kx = dt * jnp.abs(cx)
    ky = dt * jnp.abs(cy)
    kz = dt * jnp.abs(cz)
    sub = lax.broadcasted_iota(jnp.int32, (BS, HALF), 0)
    for half in range(2):
        lanes = slice(half * HALF, (half + 1) * HALF)
        _, edge = upwind_edge(cz[:, lanes], sub)
        side = edge.astype(F32)
        up64 = jnp.broadcast_to(cz[:, lanes] > 0, (GROUPS, HALF))
        ghost_z[half] = kz[:, lanes] * jnp.where(up64, pick(face[4], 2, half), pick(face[5], 2, half))
        gy = ky[:, lanes] * pick(face[3 - half], 1, half)
        gx = kx * pick(face_x, 0, half)
        for i in range(BS):
            for j in range(BS):
                group = i * BS + j
                at = slice(group * BS, (group + 1) * BS)
                z_ghost = jnp.broadcast_to(ghost_z[half, group : group + 1], (BS, HALF))
                value = inner[half, at] + side * z_ghost
                if j == (BS - 1 if half == 0 else 0):
                    value = value + gy[i * BS : (i + 1) * BS]
                advected[half, at] = value
        rows = pl.ds(first, GROUPS)
        advected[half, rows] = advected[half, rows] + gx


def bfloat_pieces(value):
    pieces = []
    for _ in range(3):
        piece = value.astype(jnp.bfloat16).astype(F32)
        pieces.append(piece)
        value = value - piece
    return pieces


def coefficient_kernel(gathered, solid, turned):
    sums = [None] * 4
    for a in range(NVX // 2, NVX):
        ca = (a - centre) * velocity_step
        high, low = gathered[a], gathered[NVX - 1 - a]
        even, odd = high + low, high - low
        terms = [even, ca * odd, ca**2 * even, ca**3 * odd]
        sums = [t if s is None else s + t for s, t in zip(sums, terms)]

    def row(n, r):
        return sums[n][r : r + 1, :]

    rho = row(0, 0)
    jx, jy, jz = row(1, 0), row(0, 1), row(0, 2)
    pxx, pyy, pzz = row(2, 0), row(0, 3), row(0, 4)
    pxy, pxz, pyz = row(1, 1), row(1, 2), row(0, 5)
    hx = row(3, 0) + row(1, 3) + row(1, 4)
    hy = row(2, 1) + row(0, 6)
    hz = row(2, 2) + row(0, 7)
    energy = pxx + pyy + pzz
    inverse = 1.0 / rho
    ux, uy, uz = jx * inverse, jy * inverse, jz * inverse
    speed = ux * ux + uy * uy + uz * uz
    temperature = (energy * inverse - speed) / 3.0
    twice = 2.0 * rho * speed - energy
    qx = hx - 2.0 * (ux * pxx + uy * pxy + uz * pxz) + ux * twice
    qy = hy - 2.0 * (ux * pxy + uy * pyy + uz * pyz) + uy * twice
    qz = hz - 2.0 * (ux * pxz + uy * pyz + uz * pzz) + uz * twice
    log_t = jnp.log(temperature)
    cold = 1.0 / temperature
    rate = (dt / rarefaction_ratio) * rho * jnp.exp(viscosity_exponent * log_t)
    keep = 1.0 / (1.0 + rate)
    amount = rate * keep * rho * (2.0 * math.pi) ** (-1.5) * jnp.exp(-1.5 * log_t)
    scale = ((1.0 - diffusivity_ratio) / 5.0) * inverse * cold * cold
    cx = own_cx()
    rx = cx - ux
    slope = -0.5 * cold
    sy, sz = qy * scale, qz * scale
    inside = solid[...] == 1
    wall_amount = 20.0 * (2.0 * math.pi * 2.0) ** (-1.5)
    rows = [
        jnp.where(inside, -0.25, slope),
        jnp.where(inside, 0.0, cold * uy),
        jnp.where(inside, 0.0, cold * uz),
        jnp.where(inside, -0.25 * (cx * cx), slope * (rx * rx + uy * uy + uz * uz)),
        jnp.where(inside, 0.0, sy),
        jnp.where(inside, 0.0, sz),
        jnp.where(inside, 0.0, rx * qx * scale - sy * uy - sz * uz),
        jnp.where(inside, 0.0, keep),
        jnp.where(inside, wall_amount, amount),
    ]
    rows = rows + [jnp.zeros_like(rho)] * (NVX - len(rows))
    pieces = jnp.concatenate(bfloat_pieces(jnp.concatenate(rows, axis=0)), axis=0)
    turned[...] = pieces.T.astype(jnp.bfloat16)


def collide(turned, basis, advected, sizes, store):
    first = 0
    for chunk in sizes:
        at = slice(first, first + chunk)
        wide = jnp.dot(turned[at], basis[...], preferred_element_type=F32)
        stay = wide[:, 2 * LANES : 2 * LANES + HALF]
        top = wide[:, 2 * LANES + HALF :]
        for half in range(2):
            exponent = wide[:, half * HALF : (half + 1) * HALF]
            flow = wide[:, LANES + half * HALF : LANES + (half + 1) * HALF]
            shape = 1.0 + flow * (-2.0 * exponent - 5.0)
            value = stay * advected[half, at] + top * jnp.exp(exponent) * shape
            store(half, first, chunk, value)
        first += chunk


def collide_kernel(
    turned, basis, neighbours, inner, own, below, above, filled, faces, flux, advected, ghost_z
):
    def store(half, first, count, value):
        filled[half, first : first + count] = value

    add_ghosts(neighbours, inner, own, below, above, advected, ghost_z)
    collide(turned, basis, advected, [PIECE] * PIECES, store)
    store_faces(filled, faces)
    face_flux(faces, flux)


def last_kernel(
    turned, basis, neighbours, inner, own, below, above, result, advected, ghost_z, out, sems
):
    copies = []

    def store(half, first, count, value):
        out[first : first + count, half * HALF : (half + 1) * HALF] = value
        if half == 1:
            at = pl.ds(first, count)
            copy = pltpu.make_async_copy(out.at[at], result.at[at], sems.at[len(copies)])
            copy.start()
            copies.append(copy)

    add_ghosts(neighbours, inner, own, below, above, advected, ghost_z)
    collide(turned, basis, advected, LAST_SIZES, store)
    for copy in copies:
        copy.wait()


VMEM = pl.BlockSpec(memory_space=pltpu.VMEM)
HBM = pl.BlockSpec(memory_space=pltpu.HBM)
FIELD = jax.ShapeDtypeStruct((2, CELLS, HALF), F32)
RESULT = jax.ShapeDtypeStruct((CELLS, LANES), F32)
FACES = jax.ShapeDtypeStruct((2, 3, GROUPS, HALF), F32)
SPREAD = jax.ShapeDtypeStruct((6 * GROUPS, CELLS), jnp.bfloat16)
FLUX = jax.ShapeDtypeStruct((3, BS, 2 * GROUPS), F32)
LOCAL = jax.ShapeDtypeStruct((BS, CELLS), F32)
SOLID = jax.ShapeDtypeStruct((1, CELLS), jnp.int32)
TABLE = jax.ShapeDtypeStruct((1, 6), jnp.int32)
PARTIAL = jax.ShapeDtypeStruct((NVX, BS, CELLS), F32)
LAST_SIZES = (176, 160, 112, 64)
BASIS = jax.ShapeDtypeStruct((3 * NVX, 3 * LANES), jnp.bfloat16)
TURNED = jax.ShapeDtypeStruct((CELLS, 3 * NVX), jnp.bfloat16)


def call(kernel, ins, outs, scratch=(), out_spec=VMEM):
    size = CELLS * LANES
    return pl.pallas_call(
        kernel,
        in_specs=ins,
        out_specs=[out_spec] * len(outs),
        out_shape=outs,
        scratch_shapes=list(scratch),
        cost_estimate=pl.CostEstimate(
            flops=40 * size, transcendentals=size, bytes_accessed=8 * size
        ),
        compiler_params=pltpu.CompilerParams(vmem_limit_bytes=16 * 1024 * 1024),
    )


def on_device(dist, neighbours, solid):
    count = lax.axis_size("space")
    forward = [(i, (i + 1) % count) for i in range(count)]
    backward = [(target, source) for source, target in forward]
    filled, faces, flux, solid, neighbours = call(
        fill_kernel,
        [HBM] * 3,
        [FIELD, FACES, FLUX, SOLID, TABLE],
        [pltpu.VMEM((CELLS, LANES), F32), pltpu.SemaphoreType.DMA((3,))],
    )(
        pltpu.with_memory_space_constraint(dist[0], pltpu.HBM),
        pltpu.with_memory_space_constraint(solid, pltpu.HBM),
        pltpu.with_memory_space_constraint(neighbours, pltpu.HBM),
    )
    for step in range(ITERS):
        flux_below = lax.ppermute(flux, "space", forward)
        below = lax.ppermute(faces, "space", forward)
        flux_above = lax.ppermute(flux, "space", backward)
        above = lax.ppermute(faces, "space", backward)
        if step == 0:
            inner, local, basis, spread, open_flux = call(
                first_inner_kernel, [VMEM], [FIELD, LOCAL, BASIS, SPREAD, FLUX]
            )(filled)
        else:
            inner, local = call(inner_kernel, [VMEM], [FIELD, LOCAL])(filled)
        (partial,) = call(join_kernel, [VMEM] * 7, [PARTIAL])(
            neighbours, local, flux, flux_below, flux_above, open_flux, spread
        )
        gathered = lax.all_to_all(partial, "vel", 0, 0, tiled=True)
        (turned,) = call(coefficient_kernel, [VMEM] * 2, [TURNED])(gathered, solid)
        operands = (turned, basis, neighbours, inner, faces, below, above)
        room = [pltpu.VMEM((2, CELLS, HALF), F32), pltpu.VMEM((2, GROUPS, HALF), F32)]
        if step < ITERS - 1:
            filled, faces, flux = call(collide_kernel, [VMEM] * 7, [FIELD, FACES, FLUX], room)(
                *operands
            )
        else:
            room = room + [pltpu.VMEM((CELLS, LANES), F32), pltpu.SemaphoreType.DMA((4,))]
            (filled,) = call(last_kernel, [VMEM] * 7, [RESULT], room, HBM)(*operands)
    return filled[None]


def solution(mesh):
    in_specs = (P("space", None, "vel"), P("space", None), P("space", None))
    out_specs = P("space", None, "vel")
    return jax.shard_map(
        on_device, mesh=mesh, in_specs=in_specs, out_specs=out_specs, check_vma=False
    )
```

```python
import math

import jax
import jax.numpy as jnp
from jax import lax
from jax.experimental import pallas as pl
from jax.experimental.pallas import tpu as pltpu
from jax.sharding import PartitionSpec as P


NVX = 16
BS = 8
ITERS = 2
CELLS = BS * BS * BS
GROUPS = BS * BS
LANES = NVX * NVX
HALF = LANES // 2

velocity_step = 0.5
diffusivity_ratio = 2.0 / 3.0
viscosity_exponent = 0.19
rarefaction_ratio = 100.0
courant = 0.9
dt = courant / (1.5 * (NVX - 1) * velocity_step)
weight = velocity_step**3
centre = (NVX - 1) / 2.0

F32 = jnp.float32


def lane_velocities(rows=1):
    lane = lax.broadcasted_iota(jnp.int32, (rows, LANES), 1)
    cy = ((lane >> 4).astype(F32) - centre) * velocity_step
    cz = ((lane & (NVX - 1)).astype(F32) - centre) * velocity_step
    return cy, cz


def own_cx():
    return (lax.axis_index("vel").astype(F32) - centre) * velocity_step


def maxwellian(rho, ux, temperature, cx, cy, cz):
    width = (cx - ux) * (cx - ux) + cy * cy + cz * cz
    return rho * (2.0 * math.pi * temperature) ** (-1.5) * jnp.exp(width * (-0.5 / temperature))


def store_faces(filled, faces):
    _, cz = lane_velocities(GROUPS)
    positive = lax.axis_index("vel") >= NVX // 2
    first = pl.multiple_of(jnp.where(positive, (BS - 1) * GROUPS, 0), GROUPS)
    for half in range(2):
        faces[half, 0] = filled[half, pl.ds(first, GROUPS), :]
        for i in range(BS):
            row = i * GROUPS + half * (BS - 1) * BS
            faces[half, 1, i * BS : (i + 1) * BS, :] = filled[half, row : row + BS, :]
        bottom = filled[half, pl.ds(0, GROUPS, stride=BS), :]
        top = filled[half, pl.ds(BS - 1, GROUPS, stride=BS), :]
        upward = cz[:, half * HALF : (half + 1) * HALF] > 0
        faces[half, 2] = jnp.where(upward, top, bottom)


PIECES = 4
PIECE = CELLS // PIECES


def two_pieces(value):
    high = value.astype(jnp.bfloat16)
    return high, (value - high.astype(F32)).astype(jnp.bfloat16)


def moment_table():
    cy, cz = lane_velocities()
    plane = cy * cy + cz * cz
    table = weight * jnp.concatenate(
        [jnp.ones_like(cy), cy, cz, cy * cy, cz * cz, cy * cz, cy * plane, cz * plane], axis=0
    )
    return jnp.concatenate([piece.astype(F32) for piece in two_pieces(table)], axis=0)


def times_transposed(table, value):
    total = None
    for piece in two_pieces(value):
        term = lax.dot_general(
            table, piece, (((1,), (1,)), ((), ())), preferred_element_type=F32
        )
        total = term if total is None else total + term
    return total


def flux_tables():
    speeds = [dt * jnp.abs(c) for c in (own_cx(), *lane_velocities())]
    _, cz = lane_velocities()
    table = moment_table()
    rising = jnp.broadcast_to(cz > 0, table.shape)
    both = [jnp.where(rising, table, 0.0), jnp.where(rising, 0.0, table)]
    return speeds, jnp.concatenate(both, axis=0).astype(jnp.bfloat16)


def flux_moments(layer, flux, tables):
    (kx, ky, kz), both = tables
    ups, downs = [], []
    for half in range(2):
        lanes = slice(half * HALF, (half + 1) * HALF)
        rows = jnp.concatenate(
            [layer(half, 0) * kx, layer(half, 1) * ky[:, lanes], layer(half, 2) * kz[:, lanes]],
            axis=0,
        )
        term = times_transposed(both[:, lanes], rows)
        ups.append(term[0:BS] + term[BS : 2 * BS])
        downs.append(term[2 * BS : 3 * BS] + term[3 * BS :])
    sums = [up + down for up, down in zip(ups, downs)]
    along_x = (sums[0] + sums[1])[:, :GROUPS]
    flux[0, :, :GROUPS] = along_x
    flux[0, :, GROUPS:] = jnp.zeros_like(along_x)
    flux[1, :, :GROUPS] = sums[0][:, GROUPS : 2 * GROUPS]
    flux[1, :, GROUPS:] = sums[1][:, GROUPS : 2 * GROUPS]
    flux[2, :, :GROUPS] = (ups[0] + ups[1])[:, 2 * GROUPS :]
    flux[2, :, GROUPS:] = (downs[0] + downs[1])[:, 2 * GROUPS :]


def face_flux(faces, flux, tables):
    flux_moments(lambda half, dim: faces[half, dim], flux, tables)


def fill_kernel(
    dist_hbm, solid_hbm, table_hbm, filled, faces, flux, solid, neighbours, dist, sems
):
    copies = [
        pltpu.make_async_copy(dist_hbm, dist, sems.at[0]),
        pltpu.make_async_copy(solid_hbm, solid, sems.at[1]),
        pltpu.make_async_copy(table_hbm, neighbours, sems.at[2]),
    ]
    for copy in copies:
        copy.start()
    cx = own_cx()
    cy, cz = lane_velocities()
    wall = maxwellian(20.0, 0.0, 2.0, cx, cy, cz)
    top = lax.broadcasted_iota(jnp.int32, (BS, HALF), 0) == 0
    tables = flux_tables()
    copies[1].wait()
    flags = jnp.broadcast_to(solid[...].astype(F32), (BS, CELLS))
    mask = lax.dot_general(
        flags, top.astype(F32), (((0,), (0,)), ((), ())), preferred_element_type=F32
    )
    inside = mask > 0.5
    copies[0].wait()
    for half in range(2):
        lanes = slice(half * HALF, (half + 1) * HALF)
        filled[half] = jnp.where(inside, wall[:, lanes], dist[:, lanes])
    store_faces(filled, faces)
    face_flux(faces, flux, tables)
    copies[2].wait()


def upwind_edge(cz, sub):
    upward = jnp.broadcast_to(cz > 0, (BS, HALF))
    return upward, (sub == 0) & upward | (sub == BS - 1) & jnp.logical_not(upward)


def cell_basis():
    cy, cz = lane_velocities(NVX)
    row = lax.broadcasted_iota(jnp.int32, (NVX, LANES), 0)
    zero = jnp.zeros((NVX, LANES), F32)

    def rows(first, entries):
        out = zero
        for k, entry in enumerate(entries):
            out = jnp.where(row == first + k, entry, out)
        return out

    exponent = rows(0, [cy * cy + cz * cz, cy, cz, 1.0])
    flow = rows(4, [cy, cz, 1.0])
    stay = rows(7, [1.0])[:, :HALF]
    top = rows(8, [1.0])[:, :HALF]
    block = jnp.concatenate([exponent, flow, stay, top], axis=1)
    return jnp.concatenate([block] * 3, axis=0).astype(jnp.bfloat16)


def first_inner_kernel(filled, inner, local, basis, open_flux):
    basis[...] = cell_basis()
    cy, cz = lane_velocities()
    inflow = maxwellian(20.0, 2.5, 1.0, own_cx(), cy, cz)
    wide = jnp.broadcast_to(inflow, (GROUPS, LANES))
    flux_moments(
        lambda half, dim: wide[:, half * HALF : (half + 1) * HALF], open_flux, flux_tables()
    )
    inner_kernel(filled, inner, local)


def inner_kernel(filled, inner, local):
    cx = own_cx()
    cy, cz = lane_velocities()
    positive = lax.axis_index("vel") >= NVX // 2
    kx = dt * jnp.abs(cx)
    ky = dt * jnp.abs(cy)
    kz = dt * jnp.abs(cz)
    keep = 1.0 - kx - ky - kz
    sub = lax.broadcasted_iota(jnp.int32, (BS, HALF), 0)
    for half in range(2):
        lanes = slice(half * HALF, (half + 1) * HALF)
        upward, edge = upwind_edge(cz[:, lanes], sub)
        k0 = jnp.broadcast_to(keep[:, lanes], (BS, HALF))
        k2 = jnp.broadcast_to(ky[:, lanes], (BS, HALF))
        k3 = jnp.where(edge, 0.0, jnp.broadcast_to(kz[:, lanes], (BS, HALF)))
        low_x = jnp.where(positive, kx, 0.0)
        high_x = jnp.where(positive, 0.0, kx)
        for i in range(BS):
            for j in range(BS):
                row = (i * BS + j) * BS
                value = filled[half, row : row + BS]
                total = k0 * value
                if i > 0:
                    total = total + low_x * filled[half, row - GROUPS : row - GROUPS + BS]
                if i < BS - 1:
                    total = total + high_x * filled[half, row + GROUPS : row + GROUPS + BS]
                if half == 0 and j < BS - 1:
                    total = total + k2 * filled[half, row + BS : row + 2 * BS]
                if half == 1 and j > 0:
                    total = total + k2 * filled[half, row - BS : row]
                z_up = jnp.where(upward, pltpu.roll(value, 1, 0), pltpu.roll(value, BS - 1, 0))
                inner[half, row : row + BS] = total + k3 * z_up
    table = moment_table().astype(jnp.bfloat16)
    total = times_transposed(table[:, :HALF], inner[0])
    total = total + times_transposed(table[:, HALF:], inner[1])
    local[...] = total[:BS] + total[BS:]


def source_places(neighbours):
    block = neighbours[...]
    here = lax.axis_index("space")
    count = lax.axis_size("space")
    places = jnp.where(block < 0, 3, lax.rem(block - here + 1 + count, count))
    face = [places[:, k : k + 1] for k in range(6)]
    positive = lax.axis_index("vel") >= NVX // 2
    return face, jnp.where(positive, face[0], face[1])


def choose(place, below, own, above, opened):
    value = jnp.where(place == 0, below, above)
    value = jnp.where(place == 1, own, value)
    return jnp.where(place == 3, opened, value)


def join_kernel(neighbours, local, own, below, above, opened, partial):
    face, face_x = source_places(neighbours)
    positive = lax.axis_index("vel") >= NVX // 2
    lane = lax.broadcasted_iota(jnp.int32, (BS, 2 * GROUPS), 1)
    early = lane < GROUPS
    places = [
        jnp.broadcast_to(face_x, early.shape),
        jnp.where(early, face[3], face[2]),
        jnp.where(early, face[4], face[5]),
    ]
    along_x, along_y, along_z = [
        choose(place, below[dim], own[dim], above[dim], opened[dim])
        for dim, place in enumerate(places)
    ]

    def spread(value, source, where):
        moved = jnp.take_along_axis(value, source, axis=1, mode="promise_in_bounds")
        return jnp.where(where, moved, 0.0)

    j, l = (lane >> 3) & (BS - 1), lane & (BS - 1)
    for pair in range(BS // 2):
        i = 2 * pair + (lane >> 6)
        at_x = i == jnp.where(positive, 0, BS - 1)
        total = spread(along_x, lane & (GROUPS - 1), at_x)
        low, high = j == 0, j == BS - 1
        total = total + spread(along_y, i * BS + l + jnp.where(low, GROUPS, 0), low | high)
        low, high = l == 0, l == BS - 1
        total = total + spread(along_z, i * BS + j + jnp.where(high, GROUPS, 0), low | high)
        cells = slice(pair * 2 * GROUPS, (pair + 1) * 2 * GROUPS)
        total = total + local[:, cells]
        partial[:, :, cells] = jnp.broadcast_to(total, (NVX, BS, 2 * GROUPS))


def add_ghosts(neighbours, inner, own, below, above, advected, ghost_z):
    cx = own_cx()
    cy, cz = lane_velocities()
    inflow = maxwellian(20.0, 2.5, 1.0, cx, cy, cz)
    face, face_x = source_places(neighbours)

    def pick(place, dim, half):
        place = jnp.broadcast_to(place, (GROUPS, HALF))
        opened = inflow[:, half * HALF : (half + 1) * HALF]
        return choose(place, below[half, dim], own[half, dim], above[half, dim], opened)

    positive = lax.axis_index("vel") >= NVX // 2
    first = pl.multiple_of(jnp.where(positive, 0, (BS - 1) * GROUPS), GROUPS)
    kx = dt * jnp.abs(cx)
    ky = dt * jnp.abs(cy)
    kz = dt * jnp.abs(cz)
    sub = lax.broadcasted_iota(jnp.int32, (BS, HALF), 0)
    for half in range(2):
        lanes = slice(half * HALF, (half + 1) * HALF)
        _, edge = upwind_edge(cz[:, lanes], sub)
        side = edge.astype(F32)
        up64 = jnp.broadcast_to(cz[:, lanes] > 0, (GROUPS, HALF))
        ghost_z[half] = kz[:, lanes] * jnp.where(up64, pick(face[4], 2, half), pick(face[5], 2, half))
        gy = ky[:, lanes] * pick(face[3 - half], 1, half)
        gx = kx * pick(face_x, 0, half)
        for i in range(BS):
            for j in range(BS):
                group = i * BS + j
                at = slice(group * BS, (group + 1) * BS)
                z_ghost = jnp.broadcast_to(ghost_z[half, group : group + 1], (BS, HALF))
                value = inner[half, at] + side * z_ghost
                if j == (BS - 1 if half == 0 else 0):
                    value = value + gy[i * BS : (i + 1) * BS]
                advected[half, at] = value
        rows = pl.ds(first, GROUPS)
        advected[half, rows] = advected[half, rows] + gx


def bfloat_pieces(value):
    pieces = []
    for _ in range(3):
        piece = value.astype(jnp.bfloat16).astype(F32)
        pieces.append(piece)
        value = value - piece
    return pieces


def coefficient_kernel(gathered, solid, turned):
    sums = [None] * 4
    for a in range(NVX // 2, NVX):
        ca = (a - centre) * velocity_step
        high, low = gathered[a], gathered[NVX - 1 - a]
        even, odd = high + low, high - low
        terms = [even, ca * odd, ca**2 * even, ca**3 * odd]
        sums = [t if s is None else s + t for s, t in zip(sums, terms)]

    def row(n, r):
        return sums[n][r : r + 1, :]

    rho = row(0, 0)
    jx, jy, jz = row(1, 0), row(0, 1), row(0, 2)
    pxx, pyy, pzz = row(2, 0), row(0, 3), row(0, 4)
    pxy, pxz, pyz = row(1, 1), row(1, 2), row(0, 5)
    hx = row(3, 0) + row(1, 3) + row(1, 4)
    hy = row(2, 1) + row(0, 6)
    hz = row(2, 2) + row(0, 7)
    energy = pxx + pyy + pzz
    inverse = 1.0 / rho
    ux, uy, uz = jx * inverse, jy * inverse, jz * inverse
    speed = ux * ux + uy * uy + uz * uz
    temperature = (energy * inverse - speed) / 3.0
    twice = 2.0 * rho * speed - energy
    qx = hx - 2.0 * (ux * pxx + uy * pxy + uz * pxz) + ux * twice
    qy = hy - 2.0 * (ux * pxy + uy * pyy + uz * pyz) + uy * twice
    qz = hz - 2.0 * (ux * pxz + uy * pyz + uz * pzz) + uz * twice
    log_t = jnp.log(temperature)
    cold = 1.0 / temperature
    rate = (dt / rarefaction_ratio) * rho * jnp.exp(viscosity_exponent * log_t)
    keep = 1.0 / (1.0 + rate)
    amount = rate * keep * rho * (2.0 * math.pi) ** (-1.5) * jnp.exp(-1.5 * log_t)
    scale = ((1.0 - diffusivity_ratio) / 5.0) * inverse * cold * cold
    cx = own_cx()
    rx = cx - ux
    slope = -0.5 * cold
    sy, sz = qy * scale, qz * scale
    inside = solid[...] == 1
    wall_amount = 20.0 * (2.0 * math.pi * 2.0) ** (-1.5)
    rows = [
        jnp.where(inside, -0.25, slope),
        jnp.where(inside, 0.0, cold * uy),
        jnp.where(inside, 0.0, cold * uz),
        jnp.where(inside, -0.25 * (cx * cx), slope * (rx * rx + uy * uy + uz * uz)),
        jnp.where(inside, 0.0, sy),
        jnp.where(inside, 0.0, sz),
        jnp.where(inside, 0.0, rx * qx * scale - sy * uy - sz * uz),
        jnp.where(inside, 0.0, keep),
        jnp.where(inside, wall_amount, amount),
    ]
    rows = rows + [jnp.zeros_like(rho)] * (NVX - len(rows))
    pieces = jnp.concatenate(bfloat_pieces(jnp.concatenate(rows, axis=0)), axis=0)
    turned[...] = pieces.T.astype(jnp.bfloat16)


def collide(turned, basis, advected, sizes, store):
    first = 0
    for chunk in sizes:
        at = slice(first, first + chunk)
        wide = jnp.dot(turned[at], basis[...], preferred_element_type=F32)
        stay = wide[:, 2 * LANES : 2 * LANES + HALF]
        top = wide[:, 2 * LANES + HALF :]
        for half in range(2):
            exponent = wide[:, half * HALF : (half + 1) * HALF]
            flow = wide[:, LANES + half * HALF : LANES + (half + 1) * HALF]
            shape = 1.0 + flow * (-2.0 * exponent - 5.0)
            value = stay * advected[half, at] + top * jnp.exp(exponent) * shape
            store(half, first, chunk, value)
        first += chunk


def collide_kernel(
    turned, basis, neighbours, inner, own, below, above, filled, faces, flux, advected, ghost_z
):
    def store(half, first, count, value):
        filled[half, first : first + count] = value

    add_ghosts(neighbours, inner, own, below, above, advected, ghost_z)
    collide(turned, basis, advected, [PIECE] * PIECES, store)
    store_faces(filled, faces)
    face_flux(faces, flux, flux_tables())


def last_kernel(
    turned, basis, neighbours, inner, own, below, above, result, advected, ghost_z, out, sems
):
    copies = []

    def store(half, first, count, value):
        out[first : first + count, half * HALF : (half + 1) * HALF] = value
        if half == 1:
            at = pl.ds(first, count)
            copy = pltpu.make_async_copy(out.at[at], result.at[at], sems.at[len(copies)])
            copy.start()
            copies.append(copy)

    add_ghosts(neighbours, inner, own, below, above, advected, ghost_z)
    collide(turned, basis, advected, LAST_SIZES, store)
    for copy in copies:
        copy.wait()


VMEM = pl.BlockSpec(memory_space=pltpu.VMEM)
HBM = pl.BlockSpec(memory_space=pltpu.HBM)
FIELD = jax.ShapeDtypeStruct((2, CELLS, HALF), F32)
RESULT = jax.ShapeDtypeStruct((CELLS, LANES), F32)
FACES = jax.ShapeDtypeStruct((2, 3, GROUPS, HALF), F32)
FLUX = jax.ShapeDtypeStruct((3, BS, 2 * GROUPS), F32)
LOCAL = jax.ShapeDtypeStruct((BS, CELLS), F32)
SOLID = jax.ShapeDtypeStruct((1, CELLS), jnp.int32)
TABLE = jax.ShapeDtypeStruct((1, 6), jnp.int32)
PARTIAL = jax.ShapeDtypeStruct((NVX, BS, CELLS), F32)
LAST_SIZES = (176, 160, 112, 64)
BASIS = jax.ShapeDtypeStruct((3 * NVX, 3 * LANES), jnp.bfloat16)
TURNED = jax.ShapeDtypeStruct((CELLS, 3 * NVX), jnp.bfloat16)


def call(kernel, ins, outs, scratch=(), out_spec=VMEM):
    size = CELLS * LANES
    return pl.pallas_call(
        kernel,
        in_specs=ins,
        out_specs=[out_spec] * len(outs),
        out_shape=outs,
        scratch_shapes=list(scratch),
        cost_estimate=pl.CostEstimate(
            flops=40 * size, transcendentals=size, bytes_accessed=8 * size
        ),
        compiler_params=pltpu.CompilerParams(vmem_limit_bytes=16 * 1024 * 1024),
    )


def on_device(dist, neighbours, solid):
    count = lax.axis_size("space")
    forward = [(i, (i + 1) % count) for i in range(count)]
    backward = [(target, source) for source, target in forward]
    filled, faces, flux, solid, neighbours = call(
        fill_kernel,
        [HBM] * 3,
        [FIELD, FACES, FLUX, SOLID, TABLE],
        [pltpu.VMEM((CELLS, LANES), F32), pltpu.SemaphoreType.DMA((3,))],
    )(
        pltpu.with_memory_space_constraint(dist[0], pltpu.HBM),
        pltpu.with_memory_space_constraint(solid, pltpu.HBM),
        pltpu.with_memory_space_constraint(neighbours, pltpu.HBM),
    )
    for step in range(ITERS):
        flux_below = lax.ppermute(flux, "space", forward)
        below = lax.ppermute(faces, "space", forward)
        flux_above = lax.ppermute(flux, "space", backward)
        above = lax.ppermute(faces, "space", backward)
        if step == 0:
            inner, local, basis, open_flux = call(
                first_inner_kernel, [VMEM], [FIELD, LOCAL, BASIS, FLUX]
            )(filled)
        else:
            inner, local = call(inner_kernel, [VMEM], [FIELD, LOCAL])(filled)
        (partial,) = call(join_kernel, [VMEM] * 6, [PARTIAL])(
            neighbours, local, flux, flux_below, flux_above, open_flux
        )
        gathered = lax.all_to_all(partial, "vel", 0, 0, tiled=True)
        (turned,) = call(coefficient_kernel, [VMEM] * 2, [TURNED])(gathered, solid)
        operands = (turned, basis, neighbours, inner, faces, below, above)
        room = [pltpu.VMEM((2, CELLS, HALF), F32), pltpu.VMEM((2, GROUPS, HALF), F32)]
        if step < ITERS - 1:
            filled, faces, flux = call(collide_kernel, [VMEM] * 7, [FIELD, FACES, FLUX], room)(
                *operands
            )
        else:
            room = room + [pltpu.VMEM((CELLS, LANES), F32), pltpu.SemaphoreType.DMA((4,))]
            (filled,) = call(last_kernel, [VMEM] * 7, [RESULT], room, HBM)(*operands)
    return filled[None]


def solution(mesh):
    in_specs = (P("space", None, "vel"), P("space", None), P("space", None))
    out_specs = P("space", None, "vel")
    return jax.shard_map(
        on_device, mesh=mesh, in_specs=in_specs, out_specs=out_specs, check_vma=False
    )
```

```python
import math

import jax
import jax.numpy as jnp
from jax import lax
from jax.experimental import pallas as pl
from jax.experimental.pallas import tpu as pltpu
from jax.sharding import PartitionSpec as P


NVX = 16
BS = 8
ITERS = 2
CELLS = BS * BS * BS
GROUPS = BS * BS
LANES = NVX * NVX
HALF = LANES // 2

velocity_step = 0.5
diffusivity_ratio = 2.0 / 3.0
viscosity_exponent = 0.19
rarefaction_ratio = 100.0
courant = 0.9
dt = courant / (1.5 * (NVX - 1) * velocity_step)
weight = velocity_step**3
centre = (NVX - 1) / 2.0

F32 = jnp.float32


def lane_velocities(rows=1):
    lane = lax.broadcasted_iota(jnp.int32, (rows, LANES), 1)
    cy = ((lane >> 4).astype(F32) - centre) * velocity_step
    cz = ((lane & (NVX - 1)).astype(F32) - centre) * velocity_step
    return cy, cz


def own_cx():
    return (lax.axis_index("vel").astype(F32) - centre) * velocity_step


def maxwellian(rho, ux, temperature, cx, cy, cz):
    width = (cx - ux) * (cx - ux) + cy * cy + cz * cz
    return rho * (2.0 * math.pi * temperature) ** (-1.5) * jnp.exp(width * (-0.5 / temperature))


def store_faces(filled, faces):
    _, cz = lane_velocities(GROUPS)
    positive = lax.axis_index("vel") >= NVX // 2
    first = pl.multiple_of(jnp.where(positive, (BS - 1) * GROUPS, 0), GROUPS)
    for half in range(2):
        faces[half, 0] = filled[half, pl.ds(first, GROUPS), :]
        for i in range(BS):
            row = i * GROUPS + half * (BS - 1) * BS
            faces[half, 1, i * BS : (i + 1) * BS, :] = filled[half, row : row + BS, :]
        bottom = filled[half, pl.ds(0, GROUPS, stride=BS), :]
        top = filled[half, pl.ds(BS - 1, GROUPS, stride=BS), :]
        upward = cz[:, half * HALF : (half + 1) * HALF] > 0
        faces[half, 2] = jnp.where(upward, top, bottom)


def two_pieces(value):
    high = value.astype(jnp.bfloat16)
    return high, (value - high.astype(F32)).astype(jnp.bfloat16)


def moment_table():
    cy, cz = lane_velocities()
    plane = cy * cy + cz * cz
    table = weight * jnp.concatenate(
        [jnp.ones_like(cy), cy, cz, cy * cy, cz * cz, cy * cz, cy * plane, cz * plane], axis=0
    )
    return jnp.concatenate([piece.astype(F32) for piece in two_pieces(table)], axis=0)


def times_transposed(table, value):
    total = None
    for piece in two_pieces(value):
        term = lax.dot_general(
            table, piece, (((1,), (1,)), ((), ())), preferred_element_type=F32
        )
        total = term if total is None else total + term
    return total


def flux_tables():
    speeds = [dt * jnp.abs(c) for c in (own_cx(), *lane_velocities())]
    _, cz = lane_velocities()
    table = moment_table()
    rising = jnp.broadcast_to(cz > 0, table.shape)
    both = [jnp.where(rising, table, 0.0), jnp.where(rising, 0.0, table)]
    return speeds, jnp.concatenate(both, axis=0).astype(jnp.bfloat16)


def flux_moments(layer, flux, tables):
    (kx, ky, kz), both = tables
    ups, downs = [], []
    for half in range(2):
        lanes = slice(half * HALF, (half + 1) * HALF)
        rows = jnp.concatenate(
            [layer(half, 0) * kx, layer(half, 1) * ky[:, lanes], layer(half, 2) * kz[:, lanes]],
            axis=0,
        )
        term = times_transposed(both[:, lanes], rows)
        ups.append(term[0:BS] + term[BS : 2 * BS])
        downs.append(term[2 * BS : 3 * BS] + term[3 * BS :])
    sums = [up + down for up, down in zip(ups, downs)]
    along_x = (sums[0] + sums[1])[:, :GROUPS]
    flux[0, :, :GROUPS] = along_x
    flux[0, :, GROUPS:] = jnp.zeros_like(along_x)
    flux[1, :, :GROUPS] = sums[0][:, GROUPS : 2 * GROUPS]
    flux[1, :, GROUPS:] = sums[1][:, GROUPS : 2 * GROUPS]
    flux[2, :, :GROUPS] = (ups[0] + ups[1])[:, 2 * GROUPS :]
    flux[2, :, GROUPS:] = (downs[0] + downs[1])[:, 2 * GROUPS :]


def face_flux(faces, flux, tables):
    flux_moments(lambda half, dim: faces[half, dim], flux, tables)


def fill_kernel(
    dist_hbm, solid_hbm, table_hbm, filled, faces, flux, solid, neighbours, dist, sems
):
    copies = [
        pltpu.make_async_copy(solid_hbm, solid, sems.at[0]),
        pltpu.make_async_copy(dist_hbm, dist, sems.at[1]),
        pltpu.make_async_copy(table_hbm, neighbours, sems.at[2]),
    ]
    for copy in copies:
        copy.start()
    cx = own_cx()
    cy, cz = lane_velocities()
    wall = maxwellian(20.0, 0.0, 2.0, cx, cy, cz)
    top = lax.broadcasted_iota(jnp.int32, (BS, HALF), 0) == 0
    tables = flux_tables()
    copies[0].wait()
    flags = jnp.broadcast_to(solid[...].astype(F32), (BS, CELLS))
    mask = lax.dot_general(
        flags, top.astype(F32), (((0,), (0,)), ((), ())), preferred_element_type=F32
    )
    inside = mask > 0.5
    copies[1].wait()
    for half in range(2):
        lanes = slice(half * HALF, (half + 1) * HALF)
        filled[half] = jnp.where(inside, wall[:, lanes], dist[:, lanes])
    store_faces(filled, faces)
    face_flux(faces, flux, tables)
    copies[2].wait()


def upwind_edge(cz, sub):
    upward = jnp.broadcast_to(cz > 0, (BS, HALF))
    return upward, (sub == 0) & upward | (sub == BS - 1) & jnp.logical_not(upward)


def cell_basis():
    cy, cz = lane_velocities(NVX)
    row = lax.broadcasted_iota(jnp.int32, (NVX, LANES), 0)
    zero = jnp.zeros((NVX, LANES), F32)

    def rows(first, entries):
        out = zero
        for k, entry in enumerate(entries):
            out = jnp.where(row == first + k, entry, out)
        return out

    exponent = rows(0, [cy * cy + cz * cz, cy, cz, 1.0])
    flow = rows(4, [cy, cz, 1.0])
    stay = rows(7, [1.0])[:, :HALF]
    top = rows(8, [1.0])[:, :HALF]
    block = jnp.concatenate([exponent, flow, stay, top], axis=1)
    return jnp.concatenate([block] * 3, axis=0).astype(jnp.bfloat16)


def first_inner_kernel(filled, inner, local, basis, open_flux):
    basis[...] = cell_basis()
    cy, cz = lane_velocities()
    inflow = maxwellian(20.0, 2.5, 1.0, own_cx(), cy, cz)
    wide = jnp.broadcast_to(inflow, (GROUPS, LANES))
    flux_moments(
        lambda half, dim: wide[:, half * HALF : (half + 1) * HALF], open_flux, flux_tables()
    )
    inner_kernel(filled, inner, local)


def inner_kernel(filled, inner, local):
    cx = own_cx()
    cy, cz = lane_velocities()
    positive = lax.axis_index("vel") >= NVX // 2
    kx = dt * jnp.abs(cx)
    ky = dt * jnp.abs(cy)
    kz = dt * jnp.abs(cz)
    keep = 1.0 - kx - ky - kz
    sub = lax.broadcasted_iota(jnp.int32, (BS, HALF), 0)
    for half in range(2):
        lanes = slice(half * HALF, (half + 1) * HALF)
        upward, edge = upwind_edge(cz[:, lanes], sub)
        k0 = jnp.broadcast_to(keep[:, lanes], (BS, HALF))
        k2 = jnp.broadcast_to(ky[:, lanes], (BS, HALF))
        k3 = jnp.where(edge, 0.0, jnp.broadcast_to(kz[:, lanes], (BS, HALF)))
        low_x = jnp.where(positive, kx, 0.0)
        high_x = jnp.where(positive, 0.0, kx)
        for i in range(BS):
            for j in range(BS):
                row = (i * BS + j) * BS
                value = filled[half, row : row + BS]
                total = k0 * value
                if i > 0:
                    total = total + low_x * filled[half, row - GROUPS : row - GROUPS + BS]
                if i < BS - 1:
                    total = total + high_x * filled[half, row + GROUPS : row + GROUPS + BS]
                if half == 0 and j < BS - 1:
                    total = total + k2 * filled[half, row + BS : row + 2 * BS]
                if half == 1 and j > 0:
                    total = total + k2 * filled[half, row - BS : row]
                z_up = jnp.where(upward, pltpu.roll(value, 1, 0), pltpu.roll(value, BS - 1, 0))
                inner[half, row : row + BS] = total + k3 * z_up
    table = moment_table().astype(jnp.bfloat16)
    total = times_transposed(table[:, :HALF], inner[0])
    total = total + times_transposed(table[:, HALF:], inner[1])
    local[...] = total[:BS] + total[BS:]


def source_places(neighbours):
    block = neighbours[...]
    here = lax.axis_index("space")
    count = lax.axis_size("space")
    places = jnp.where(block < 0, 3, lax.rem(block - here + 1 + count, count))
    face = [places[:, k : k + 1] for k in range(6)]
    positive = lax.axis_index("vel") >= NVX // 2
    return face, jnp.where(positive, face[0], face[1])


def choose(place, below, own, above, opened):
    value = jnp.where(place == 0, below, above)
    value = jnp.where(place == 1, own, value)
    return jnp.where(place == 3, opened, value)


def join_kernel(neighbours, local, own, below, above, opened, partial):
    face, face_x = source_places(neighbours)
    positive = lax.axis_index("vel") >= NVX // 2
    lane = lax.broadcasted_iota(jnp.int32, (BS, 2 * GROUPS), 1)
    early = lane < GROUPS
    places = [
        jnp.broadcast_to(face_x, early.shape),
        jnp.where(early, face[3], face[2]),
        jnp.where(early, face[4], face[5]),
    ]
    along_x, along_y, along_z = [
        choose(place, below[dim], own[dim], above[dim], opened[dim])
        for dim, place in enumerate(places)
    ]

    def spread(value, source, where):
        moved = jnp.take_along_axis(value, source, axis=1, mode="promise_in_bounds")
        return jnp.where(where, moved, 0.0)

    j, l = (lane >> 3) & (BS - 1), lane & (BS - 1)
    for pair in range(BS // 2):
        i = 2 * pair + (lane >> 6)
        at_x = i == jnp.where(positive, 0, BS - 1)
        total = spread(along_x, lane & (GROUPS - 1), at_x)
        low, high = j == 0, j == BS - 1
        total = total + spread(along_y, i * BS + l + jnp.where(low, GROUPS, 0), low | high)
        low, high = l == 0, l == BS - 1
        total = total + spread(along_z, i * BS + j + jnp.where(high, GROUPS, 0), low | high)
        cells = slice(pair * 2 * GROUPS, (pair + 1) * 2 * GROUPS)
        total = total + local[:, cells]
        partial[:, :, cells] = jnp.broadcast_to(total, (NVX, BS, 2 * GROUPS))


def add_ghosts(neighbours, inner, own, below, above, advected, ghost_z):
    cx = own_cx()
    cy, cz = lane_velocities()
    inflow = maxwellian(20.0, 2.5, 1.0, cx, cy, cz)
    face, face_x = source_places(neighbours)

    def pick(place, dim, half):
        place = jnp.broadcast_to(place, (GROUPS, HALF))
        opened = inflow[:, half * HALF : (half + 1) * HALF]
        return choose(place, below[half, dim], own[half, dim], above[half, dim], opened)

    positive = lax.axis_index("vel") >= NVX // 2
    first = pl.multiple_of(jnp.where(positive, 0, (BS - 1) * GROUPS), GROUPS)
    kx = dt * jnp.abs(cx)
    ky = dt * jnp.abs(cy)
    kz = dt * jnp.abs(cz)
    sub = lax.broadcasted_iota(jnp.int32, (BS, HALF), 0)
    for half in range(2):
        lanes = slice(half * HALF, (half + 1) * HALF)
        _, edge = upwind_edge(cz[:, lanes], sub)
        side = edge.astype(F32)
        up64 = jnp.broadcast_to(cz[:, lanes] > 0, (GROUPS, HALF))
        ghost_z[half] = kz[:, lanes] * jnp.where(up64, pick(face[4], 2, half), pick(face[5], 2, half))
        gy = ky[:, lanes] * pick(face[3 - half], 1, half)
        gx = kx * pick(face_x, 0, half)
        for i in range(BS):
            for j in range(BS):
                group = i * BS + j
                at = slice(group * BS, (group + 1) * BS)
                z_ghost = jnp.broadcast_to(ghost_z[half, group : group + 1], (BS, HALF))
                value = inner[half, at] + side * z_ghost
                if j == (BS - 1 if half == 0 else 0):
                    value = value + gy[i * BS : (i + 1) * BS]
                advected[half, at] = value
        rows = pl.ds(first, GROUPS)
        advected[half, rows] = advected[half, rows] + gx


def bfloat_pieces(value):
    pieces = []
    for _ in range(3):
        piece = value.astype(jnp.bfloat16).astype(F32)
        pieces.append(piece)
        value = value - piece
    return pieces


def coefficient_kernel(gathered, solid, turned):
    sums = [None] * 4
    for a in range(NVX // 2, NVX):
        ca = (a - centre) * velocity_step
        high, low = gathered[a], gathered[NVX - 1 - a]
        even, odd = high + low, high - low
        terms = [even, ca * odd, ca**2 * even, ca**3 * odd]
        sums = [t if s is None else s + t for s, t in zip(sums, terms)]

    def row(n, r):
        return sums[n][r : r + 1, :]

    rho = row(0, 0)
    jx, jy, jz = row(1, 0), row(0, 1), row(0, 2)
    pxx, pyy, pzz = row(2, 0), row(0, 3), row(0, 4)
    pxy, pxz, pyz = row(1, 1), row(1, 2), row(0, 5)
    hx = row(3, 0) + row(1, 3) + row(1, 4)
    hy = row(2, 1) + row(0, 6)
    hz = row(2, 2) + row(0, 7)
    energy = pxx + pyy + pzz
    inverse = 1.0 / rho
    ux, uy, uz = jx * inverse, jy * inverse, jz * inverse
    speed = ux * ux + uy * uy + uz * uz
    temperature = (energy * inverse - speed) / 3.0
    twice = 2.0 * rho * speed - energy
    qx = hx - 2.0 * (ux * pxx + uy * pxy + uz * pxz) + ux * twice
    qy = hy - 2.0 * (ux * pxy + uy * pyy + uz * pyz) + uy * twice
    qz = hz - 2.0 * (ux * pxz + uy * pyz + uz * pzz) + uz * twice
    log_t = jnp.log(temperature)
    cold = 1.0 / temperature
    rate = (dt / rarefaction_ratio) * rho * jnp.exp(viscosity_exponent * log_t)
    keep = 1.0 / (1.0 + rate)
    amount = rate * keep * rho * (2.0 * math.pi) ** (-1.5) * jnp.exp(-1.5 * log_t)
    scale = ((1.0 - diffusivity_ratio) / 5.0) * inverse * cold * cold
    cx = own_cx()
    rx = cx - ux
    slope = -0.5 * cold
    sy, sz = qy * scale, qz * scale
    inside = solid[...] == 1
    wall_amount = 20.0 * (2.0 * math.pi * 2.0) ** (-1.5)
    rows = [
        jnp.where(inside, -0.25, slope),
        jnp.where(inside, 0.0, cold * uy),
        jnp.where(inside, 0.0, cold * uz),
        jnp.where(inside, -0.25 * (cx * cx), slope * (rx * rx + uy * uy + uz * uz)),
        jnp.where(inside, 0.0, sy),
        jnp.where(inside, 0.0, sz),
        jnp.where(inside, 0.0, rx * qx * scale - sy * uy - sz * uz),
        jnp.where(inside, 0.0, keep),
        jnp.where(inside, wall_amount, amount),
    ]
    rows = rows + [jnp.zeros_like(rho)] * (NVX - len(rows))
    pieces = jnp.concatenate(bfloat_pieces(jnp.concatenate(rows, axis=0)), axis=0)
    turned[...] = pieces.T.astype(jnp.bfloat16)


def collide(turned, basis, advected, sizes, store):
    first = 0
    for chunk in sizes:
        at = slice(first, first + chunk)
        wide = jnp.dot(turned[at], basis[...], preferred_element_type=F32)
        stay = wide[:, 2 * LANES : 2 * LANES + HALF]
        top = wide[:, 2 * LANES + HALF :]
        for half in range(2):
            exponent = wide[:, half * HALF : (half + 1) * HALF]
            flow = wide[:, LANES + half * HALF : LANES + (half + 1) * HALF]
            shape = 1.0 + flow * (-2.0 * exponent - 5.0)
            value = stay * advected[half, at] + top * jnp.exp(exponent) * shape
            store(half, first, chunk, value)
        first += chunk


def collide_kernel(
    turned, basis, neighbours, inner, own, below, above, filled, faces, flux, advected, ghost_z
):
    def store(half, first, count, value):
        filled[half, first : first + count] = value

    add_ghosts(neighbours, inner, own, below, above, advected, ghost_z)
    collide(turned, basis, advected, [GROUPS] * BS, store)
    store_faces(filled, faces)
    face_flux(faces, flux, flux_tables())


def last_kernel(
    turned, basis, neighbours, inner, own, below, above, result, advected, ghost_z, out, sems
):
    copies = []

    def store(half, first, count, value):
        out[first : first + count, half * HALF : (half + 1) * HALF] = value
        if half == 1:
            at = pl.ds(first, count)
            copy = pltpu.make_async_copy(out.at[at], result.at[at], sems.at[len(copies)])
            copy.start()
            copies.append(copy)

    add_ghosts(neighbours, inner, own, below, above, advected, ghost_z)
    collide(turned, basis, advected, LAST_SIZES, store)
    for copy in copies:
        copy.wait()


VMEM = pl.BlockSpec(memory_space=pltpu.VMEM)
HBM = pl.BlockSpec(memory_space=pltpu.HBM)
FIELD = jax.ShapeDtypeStruct((2, CELLS, HALF), F32)
RESULT = jax.ShapeDtypeStruct((CELLS, LANES), F32)
FACES = jax.ShapeDtypeStruct((2, 3, GROUPS, HALF), F32)
FLUX = jax.ShapeDtypeStruct((3, BS, 2 * GROUPS), F32)
LOCAL = jax.ShapeDtypeStruct((BS, CELLS), F32)
SOLID = jax.ShapeDtypeStruct((1, CELLS), jnp.int32)
TABLE = jax.ShapeDtypeStruct((1, 6), jnp.int32)
PARTIAL = jax.ShapeDtypeStruct((NVX, BS, CELLS), F32)
LAST_SIZES = (176, 160, 112, 64)
BASIS = jax.ShapeDtypeStruct((3 * NVX, 3 * LANES), jnp.bfloat16)
TURNED = jax.ShapeDtypeStruct((CELLS, 3 * NVX), jnp.bfloat16)


def call(kernel, ins, outs, scratch=(), out_spec=VMEM):
    size = CELLS * LANES
    return pl.pallas_call(
        kernel,
        in_specs=ins,
        out_specs=[out_spec] * len(outs),
        out_shape=outs,
        scratch_shapes=list(scratch),
        cost_estimate=pl.CostEstimate(
            flops=40 * size, transcendentals=size, bytes_accessed=8 * size
        ),
        compiler_params=pltpu.CompilerParams(vmem_limit_bytes=16 * 1024 * 1024),
    )


def on_device(dist, neighbours, solid):
    count = lax.axis_size("space")
    forward = [(i, (i + 1) % count) for i in range(count)]
    backward = [(target, source) for source, target in forward]
    filled, faces, flux, solid, neighbours = call(
        fill_kernel,
        [HBM] * 3,
        [FIELD, FACES, FLUX, SOLID, TABLE],
        [pltpu.VMEM((CELLS, LANES), F32), pltpu.SemaphoreType.DMA((3,))],
    )(
        pltpu.with_memory_space_constraint(dist[0], pltpu.HBM),
        pltpu.with_memory_space_constraint(solid, pltpu.HBM),
        pltpu.with_memory_space_constraint(neighbours, pltpu.HBM),
    )
    for step in range(ITERS):
        flux_below = lax.ppermute(flux, "space", forward)
        below = lax.ppermute(faces, "space", forward)
        flux_above = lax.ppermute(flux, "space", backward)
        above = lax.ppermute(faces, "space", backward)
        if step == 0:
            inner, local, basis, open_flux = call(
                first_inner_kernel, [VMEM], [FIELD, LOCAL, BASIS, FLUX]
            )(filled)
        else:
            inner, local = call(inner_kernel, [VMEM], [FIELD, LOCAL])(filled)
        (partial,) = call(join_kernel, [VMEM] * 6, [PARTIAL])(
            neighbours, local, flux, flux_below, flux_above, open_flux
        )
        gathered = lax.all_to_all(partial, "vel", 0, 0, tiled=True)
        (turned,) = call(coefficient_kernel, [VMEM] * 2, [TURNED])(gathered, solid)
        operands = (turned, basis, neighbours, inner, faces, below, above)
        room = [pltpu.VMEM((2, CELLS, HALF), F32), pltpu.VMEM((2, GROUPS, HALF), F32)]
        if step < ITERS - 1:
            filled, faces, flux = call(collide_kernel, [VMEM] * 7, [FIELD, FACES, FLUX], room)(
                *operands
            )
        else:
            room = room + [pltpu.VMEM((CELLS, LANES), F32), pltpu.SemaphoreType.DMA((4,))]
            (filled,) = call(last_kernel, [VMEM] * 7, [RESULT], room, HBM)(*operands)
    return filled[None]


def solution(mesh):
    in_specs = (P("space", None, "vel"), P("space", None), P("space", None))
    out_specs = P("space", None, "vel")
    return jax.shard_map(
        on_device, mesh=mesh, in_specs=in_specs, out_specs=out_specs, check_vma=False
    )
```
